512 devices in a mesh: ctx: 16 (over z), exp: 32 (over x, y, core).
Axes of the slice: x: 4, y: 4, z: 16, core: 2. Of those that a mesh axis runs over, the one named last changes fastest.
Arguments:
- queries: bfloat16 [2048, 8192], P('ctx', 'exp'), may hold values from -6 to 6
- key_rows: bfloat16 [2048, 8192], P('ctx', 'exp'), may hold values from -6 to 6
- value_rows: bfloat16 [2048, 8192], P('ctx', 'exp'), may hold values from -6 to 6
- decay_rate: float32 [64], P('exp'), may hold values from 0.00024414062 to 0.04
- residual: bfloat16 [2048, 3072], P('exp', 'ctx'), may hold values from -6 to 6
- out_proj: bfloat16 [8192, 3072], P('exp', 'ctx'), may hold values from -0.0625 to 0.0625
- routes: int32 [2048, 2], P('exp'), may hold values from 0 to 15, all different within a row; in each aligned block of 64 rows (0 to 63, 64 to 127, ...) at most 16 rows name the same one
- gate_shares: int32 [2048, 2], P('exp'), may hold values from 1 to 8
- gate_proj: bfloat16 [32, 4096, 3072], P('exp', 'ctx'), may hold values from -0.109375 to 0.109375
- up_proj: bfloat16 [32, 4096, 3072], P('exp', 'ctx'), may hold values from -0.109375 to 0.109375
- down_proj: bfloat16 [32, 3072, 4096], P('exp', 'ctx'), may hold values from -0.0625 to 0.0625
Outputs:
- layer_out: bfloat16 [2048, 3072], P('exp', 'ctx')
The draws below stay inside these ranges and needn't reach their ends.
Inputs may be any that keep to these rules, and one draw needn't show every extreme that they name: `routes`: each token names 2 different experts. Among the 64 tokens of each aligned block no expert is named by more than 16 tokens, a bound that some block reaches.
All inputs are finite; a program needn't handle non-finite values.
Results may differ from the reference program's by a relative error of at most 0.017.
Values may be sent and summed in bfloat16 or wider, within the bound.
A program may use at most 64 MiB of HBM per device.

```python
import math
import jax
import jax.numpy as jnp
import numpy as np
from jax import lax

D = 3072
FF = 8192
DH = 128
TOP = 2
TOK_CTX = 128
HEADS = 64
EXPERTS = 16
TOKENS = 2048
ROWS = 64
CAP = 16
N_EXP = 32


def plant(drawn, stream_key, low, top_value):
    dims = drawn.shape
    place = [jax.random.randint(jax.random.fold_in(stream_key, axis), (), 0, dims[axis]) for axis in range(len(dims))]
    drawn = drawn.at[tuple(place)].set(low)
    longest = dims.index(max(dims))
    place[longest] = (place[longest] + 1) % dims[longest]
    return drawn.at[tuple(place)].set(top_value)


def steps_of(key, dims, cuts, low, largest):
    def one(axis_at, blocks):
        steps = jax.random.uniform(jax.random.fold_in(jax.random.fold_in(key, 6), axis_at), (blocks,), jnp.float32, low / len(cuts), largest / len(cuts))
        return jnp.repeat(jnp.exp(steps), dims[axis_at] // blocks).reshape((-1,) + (1,) * (len(dims) - axis_at - 1))

    gain = one(*cuts[0])
    for cut in cuts[1:]:
        gain = gain * one(*cut)
    return gain


def routed_block(own_key, own, number, rows, count, top, bound, skew):
    order = jax.random.permutation(own_key, count)
    packed, ordinary = load_shares(count, rows * top, bound, skew, True), load_shares(count, rows * top, bound, skew, False)
    places = jnp.arange(count)

    def named(lengths, rotation):
        used = int((lengths > 0).sum())
        fixed = max(1, used // 4)
        passed = fixed + (places - fixed + rotation * (used - fixed)) % max(1, count - fixed)
        return jnp.zeros((count,), jnp.int32).at[order[jnp.where(places < fixed, places, passed)]].set(jnp.asarray(lengths, jnp.int32))

    lengths = jnp.where(number % 4 == 0, named(packed, number // 4), named(ordinary, number - number // 4 - 1))
    mixed = jax.random.permutation(jax.random.fold_in(own, 3), count)
    giver, sink = mixed[0:count // 2 * 2:2], mixed[1:count // 2 * 2:2]
    margin = jnp.minimum(lengths[giver] - 1, bound - lengths[sink]) // 2
    margin = jnp.where((giver == order[0]) | (sink == order[0]) | (lengths[sink] == 0), 0, jnp.maximum(margin, 0))
    passed = jax.random.randint(jax.random.fold_in(own, 4), (count // 2,), 0, 1 << 20) % (margin + 1)
    lengths = lengths.at[giver].add(-passed).at[sink].add(passed)
    items = jnp.searchsorted(jnp.cumsum(lengths), jnp.arange(rows * top), side="right").astype(jnp.int32)
    listing = items.reshape(top, rows).T
    listing = listing[jax.random.permutation(jax.random.fold_in(own, 1), rows)]
    rotation = jax.random.randint(jax.random.fold_in(own, 2), (rows, 1), 0, top)
    return jnp.take_along_axis(listing, (jnp.arange(top)[None, :] + rotation) % top, axis=1)


def load_shares(number_of, total, most, slope, full):
    portions = [(1 << 20) // math.isqrt(standing ** slope) + 1 for standing in range(1, number_of + 1)]
    largest = most if full else min(most, max(-(-total // number_of), total * portions[0] // sum(portions)))
    least = 1 if total - largest >= number_of - 1 else 0
    holding, spare = [largest] + [least] * (number_of - 1), total - largest - least * (number_of - 1)
    while spare > 0:
        free = [i for i in range(1, number_of) if holding[i] < largest] or [i for i in range(1, number_of) if holding[i] < most]
        whole, remaining = sum([portions[i] for i in free]), spare
        for i in free:
            addition = min(most - holding[i], max(1, remaining * portions[i] // whole), spare)
            holding[i] = holding[i] + addition
            spare = spare - addition
    return np.array(holding)


def bell_draw(own_key, shape, deviation, reach, cuts=(), held_as=jnp.bfloat16):
    values = deviation * jax.random.normal(own_key, shape, jnp.float32)
    if cuts:
        values = values * steps_of(own_key, shape, cuts, -0.22, 0.18)
    return jnp.clip(values, -reach, reach).astype(held_as)


def setup_inputs(seed: int = 0) -> dict:
    key_list = jax.random.split(jax.random.key(seed), 12)
    queries = bell_draw(key_list[0], (TOKENS, HEADS * DH), 1.0, 6.0, ((0, 16), (1, 32)))
    key_rows = bell_draw(key_list[1], (TOKENS, HEADS * DH), 1.0, 6.0, ((0, 16), (1, 32)))
    value_rows = bell_draw(key_list[2], (TOKENS, HEADS * DH), 1.0, 6.0, ((0, 16), (1, 32)))
    decay_rate = jnp.clip(jnp.exp(math.log(0.04) - 5.0988903 * jax.random.uniform(key_list[3], (HEADS,), jnp.float32) ** steps_of(key_list[3], (HEADS,), ((0, 32),), -0.2, 0.2)), 0.00024414062, 0.04)
    residual = bell_draw(key_list[4], (TOKENS, D), 1.0, 6.0, ((0, 32), (1, 16)))
    out_proj = bell_draw(key_list[5], (HEADS * DH, D), (HEADS * DH) ** -0.5, 0.0625, ((0, 32), (1, 16)))
    routes_keys = jax.random.split(jax.random.fold_in(key_list[6], 1), TOKENS // ROWS)
    routes_turns = jax.random.permutation(jax.random.fold_in(key_list[6], 3), TOKENS // ROWS)
    routes = jax.vmap(lambda own, number: routed_block(jax.random.fold_in(key_list[6], 2), own, number, ROWS, EXPERTS, TOP, CAP, 1))(routes_keys, routes_turns).reshape((TOKENS, TOP))
    gate_shares = plant(jax.random.randint(key_list[7], (TOKENS, TOP), 1, 9), jax.random.fold_in(key_list[7], 1), 1, 8).astype(jnp.int32)
    gate_proj = bell_draw(key_list[8], (2 * EXPERTS, FF // 2, D), D ** -0.5, 0.109375, ((0, 32), (1, 16)))
    up_proj = bell_draw(key_list[9], (2 * EXPERTS, FF // 2, D), D ** -0.5, 0.109375, ((0, 32), (1, 16)))
    down_proj = bell_draw(key_list[10], (2 * EXPERTS, D, FF // 2), FF ** -0.5, 0.0625, ((0, 32), (1, 16)))
    return dict(queries=queries, key_rows=key_rows, value_rows=value_rows, decay_rate=decay_rate, residual=residual, out_proj=out_proj, routes=routes, gate_shares=gate_shares, gate_proj=gate_proj, up_proj=up_proj, down_proj=down_proj)


def rms_norm(vals):
    return vals * lax.rsqrt(lax.optimization_barrier(jnp.mean(vals * vals, axis=-1, keepdims=True)) + 1e-06)

def lightning(queries, key_rows, value_rows, decay_rate):
    heads = decay_rate.shape[0]
    width = queries.shape[1] // heads
    count = TOK_CTX
    blocks = queries.shape[0] // count
    places = jnp.arange(count, dtype=jnp.float32)
    lags = places[:, None] - places[None, :]
    inside = jnp.where(lags[None] >= 0, jnp.exp(-decay_rate[:, None, None] * jnp.maximum(lags, 0.0)[None]), 0.0)
    query_scale = jnp.exp(-decay_rate[:, None] * places[None, :]).T
    key_scale = jnp.exp(-decay_rate[:, None] * (count - places)[None, :]).T
    carry_scale = jnp.exp(-decay_rate * count)
    shaped = lambda arr: arr.reshape(blocks, count, heads, width)

    def advance(state, items):
        q_blk, k_blk, v_blk = items
        qf = q_blk.astype(jnp.float32)
        kf = k_blk.astype(jnp.float32)
        vf = v_blk.astype(jnp.float32)
        scores = jnp.einsum('thd,shd->hts', qf, kf)
        weight = (scores * inside).astype(jnp.bfloat16)
        intra = jnp.einsum('hts,shd->thd', weight.astype(jnp.float32), vf)
        inter = jnp.einsum('thd,hde->the', qf, state, precision=lax.Precision.HIGHEST) * query_scale[:, :, None]
        normed = rms_norm(intra + inter).astype(jnp.bfloat16)
        local = jnp.einsum('shd,she->hde', kf * key_scale[:, :, None], vf, precision=lax.Precision.HIGHEST)
        state = carry_scale[:, None, None] * state + local
        return (state, normed)
    start = jnp.zeros((heads, width, width), jnp.float32)
    state, outs = lax.scan(advance, start, (shaped(queries), shaped(key_rows), shaped(value_rows)))
    return outs.reshape(blocks * count, heads * width)

def reference(queries, key_rows, value_rows, decay_rate, residual, out_proj, routes, gate_shares, gate_proj, up_proj, down_proj):
    attn = lightning(queries, key_rows, value_rows, decay_rate)
    stream = (jnp.dot(attn, out_proj, preferred_element_type=jnp.float32) + residual.astype(jnp.float32)).astype(jnp.bfloat16)
    normed = rms_norm(stream.astype(jnp.float32)).astype(jnp.bfloat16)
    flat = routes.reshape(-1).astype(jnp.int32)
    limit = N_EXP * CAP
    width = stream.shape[1]
    experts = gate_proj.shape[0] // 2
    half = gate_proj.shape[1]
    contract = (((1,), (1,)), ((), ()))

    def per_expert(carry, items):
        w_gate, w_up, w_down, which = items
        w_down_full = jnp.concatenate([w_down[0], w_down[1]], axis=1)
        hits = flat == which
        picked = jnp.nonzero(hits, size=limit, fill_value=0)[0].astype(jnp.int32)
        valid = jnp.arange(limit) < jnp.sum(hits.astype(jnp.int32))
        rows_in = normed[picked // TOP]
        gate = lax.dot_general(rows_in, w_gate, contract, preferred_element_type=jnp.float32)
        upper = lax.dot_general(rows_in, w_up, contract, preferred_element_type=jnp.float32)
        hidden = (jax.nn.silu(gate) * upper).astype(jnp.bfloat16)
        result = lax.dot_general(hidden, w_down_full, contract, preferred_element_type=jnp.float32).astype(jnp.bfloat16)
        result = jnp.where(valid[:, None], result.astype(jnp.float32), 0.0)
        return (carry.at[picked].add(result), None)
    gate_all = gate_proj.reshape(experts, 2 * half, width)
    up_all = up_proj.reshape(experts, 2 * half, width)
    down_all = down_proj.reshape(experts, 2, width, half)
    start = jnp.zeros((flat.shape[0], width), jnp.float32)
    gathered, unused = lax.scan(per_expert, start, (gate_all, up_all, down_all, jnp.arange(experts, dtype=jnp.int32)))
    shares = gate_shares.astype(jnp.float32)
    shares = shares / lax.optimization_barrier(jnp.sum(shares, axis=1, keepdims=True))
    mixed = lax.optimization_barrier(jnp.sum(gathered.reshape(-1, TOP, width) * shares[:, :, None], axis=1))
    return (stream.astype(jnp.float32) + mixed).astype(jnp.bfloat16)
```

```python
import functools
import jax
import jax.numpy as jnp
from jax import lax
from jax.experimental import pallas as pl
from jax.experimental.pallas import tpu as pltpu
from jax.sharding import PartitionSpec as P

MESH = pl.DeviceIdType.MESH


def ring_kernel(n, chunks, paired, x_ref, out_ref, send, recv, own_sem, pass_send, pass_recv):
    me = lax.axis_index("ctx")
    col = lax.axis_index("exp")
    near = (lax.rem(me + 1, n), lax.rem(me + n - 1, n))
    core = lax.rem(col, 2)
    partner = col + 1 - 2 * core
    half = n // 2

    barrier = pltpu.get_barrier_semaphore()
    for peer in near:
        pl.semaphore_signal(barrier, inc=1, device_id={"ctx": peer}, device_id_type=MESH)
    if paired:
        pl.semaphore_signal(barrier, inc=1, device_id={"exp": partner}, device_id_type=MESH)
    keep = pltpu.make_async_copy(x_ref, out_ref.at[me], own_sem)
    keep.start()
    pl.semaphore_wait(barrier, 3 if paired else 2)

    def origin_of(way, step):
        return lax.rem(me - step + n, n) if way == 0 else lax.rem(me + step, n)

    def place(ref, index, chunk, side):
        lead = () if index is None else (index,)
        return ref.at[lead + ((side, chunk) if paired else (chunk,))]

    def hop(way, step, chunk):
        origin = origin_of(way, step)
        src = place(x_ref, None, chunk, core) if step == 0 else place(out_ref, origin, chunk, core)
        return pltpu.make_async_remote_copy(
            src_ref=src,
            dst_ref=place(out_ref, origin, chunk, core),
            send_sem=send.at[way, step, chunk],
            recv_sem=recv.at[way, step, chunk],
            device_id={"ctx": near[way]},
            device_id_type=MESH,
        )

    def landed(way, step, chunk):
        spot = place(out_ref, origin_of(way, step + 1), chunk, core)
        return pltpu.make_async_remote_copy(
            src_ref=spot,
            dst_ref=spot,
            send_sem=send.at[way, step, chunk],
            recv_sem=recv.at[way, step, chunk],
            device_id={"ctx": near[way]},
            device_id_type=MESH,
        )

    def across(way, step, chunk, side):
        spot = place(out_ref, origin_of(way, step + 1), chunk, side)
        return pltpu.make_async_remote_copy(
            src_ref=spot,
            dst_ref=spot,
            send_sem=pass_send.at[way, step, chunk],
            recv_sem=pass_recv.at[way, step, chunk],
            device_id={"exp": partner},
            device_id_type=MESH,
        )

    def carried(way, step, chunk):
        return step < half - 1 or (chunk < chunks // 2) == (way == 0)

    order = [(step, chunk, way) for step in range(half) for chunk in range(chunks) for way in range(2)]
    moved = [(way, step, chunk) for step, chunk, way in order if carried(way, step, chunk)]
    for step in range(half + 1):
        for chunk in range(chunks):
            for way in range(2):
                if step > 0 and carried(way, step - 1, chunk):
                    landed(way, step - 1, chunk).wait_recv()
                if step < half and carried(way, step, chunk):
                    hop(way, step, chunk).start()
                if paired and step > 0 and carried(way, step - 1, chunk):
                    across(way, step - 1, chunk, core).start()
    for item in moved:
        hop(*item).wait_send()
    if paired:
        for item in moved:
            across(*item, core).wait_send()
            across(*item, 1 - core).wait_recv()
    keep.wait()


def ring_gather(x, ident, paired=False):
    n = lax.axis_size("ctx")
    chunks = x.shape[1] if paired else x.shape[0]
    sems = pltpu.SemaphoreType.DMA((2, n // 2, chunks))
    return pl.pallas_call(
        functools.partial(ring_kernel, n, chunks, paired),
        out_shape=jax.ShapeDtypeStruct((n,) + x.shape, x.dtype),
        in_specs=[pl.BlockSpec(memory_space=pltpu.VMEM)],
        out_specs=pl.BlockSpec(memory_space=pltpu.VMEM),
        scratch_shapes=[sems, sems, pltpu.SemaphoreType.DMA, sems, sems],
        compiler_params=pltpu.CompilerParams(collective_id=ident, has_side_effects=True),
        name="ring_gather",
    )(x)


def exchange_kernel(n, share, x_ref, out_ref, send, recv, own_sem):
    me = lax.axis_index("exp")
    barrier = pltpu.get_barrier_semaphore()

    def greet(j, carry):
        pl.semaphore_signal(
            barrier, inc=1, device_id={"exp": lax.rem(me + j, n)}, device_id_type=MESH
        )
        return carry

    lax.fori_loop(1, n, greet, 0)
    keep = pltpu.make_async_copy(x_ref.at[me // share], out_ref.at[me], own_sem)
    keep.start()
    pl.semaphore_wait(barrier, n - 1)

    def outward(j):
        peer = lax.rem(me + j, n)
        return pltpu.make_async_remote_copy(
            src_ref=x_ref.at[peer // share],
            dst_ref=out_ref.at[me],
            send_sem=send.at[j],
            recv_sem=recv.at[j],
            device_id={"exp": peer},
            device_id_type=MESH,
        )

    def inward(j):
        spot = out_ref.at[lax.rem(me - j + n, n)]
        return pltpu.make_async_remote_copy(
            src_ref=spot,
            dst_ref=spot,
            send_sem=send.at[j],
            recv_sem=recv.at[j],
            device_id={"exp": lax.rem(me + j, n)},
            device_id_type=MESH,
        )

    def launch(j, carry):
        outward(j).start()
        return carry

    def finish(j, carry):
        inward(j).wait_recv()
        outward(j).wait_send()
        return carry

    lax.fori_loop(1, n, launch, 0)
    lax.fori_loop(1, n, finish, 0)
    keep.wait()


def exchange(x, ident):
    n = lax.axis_size("exp")
    sems = pltpu.SemaphoreType.DMA((n,))
    return pl.pallas_call(
        functools.partial(exchange_kernel, n, n // x.shape[0]),
        out_shape=jax.ShapeDtypeStruct((n,) + x.shape[1:], x.dtype),
        in_specs=[pl.BlockSpec(memory_space=pltpu.VMEM)],
        out_specs=pl.BlockSpec(memory_space=pltpu.VMEM),
        scratch_shapes=[sems, sems, pltpu.SemaphoreType.DMA],
        compiler_params=pltpu.CompilerParams(collective_id=ident, has_side_effects=True),
        name="exchange",
    )(x)


def rms_norm(vals, axis):
    return vals * lax.rsqrt(jnp.mean(vals * vals, axis=axis, keepdims=True) + 1e-06)


def body(
    queries,
    key_rows,
    value_rows,
    decay_rate,
    residual,
    out_proj,
    routes,
    gate_shares,
    gate_proj,
    up_proj,
    down_proj,
):
    count = queries.shape[0]
    heads = decay_rate.shape[0]
    width = queries.shape[1] // heads
    ring = lax.axis_size("ctx")
    index = lax.axis_index("ctx")
    q_blk = queries.reshape(count, heads, width)
    k_blk = key_rows.reshape(count, heads, width)
    v_blk = value_rows.reshape(count, heads, width)
    places = jnp.arange(count, dtype=jnp.float32)
    lags = places[:, None] - places[None, :]
    inside = jnp.where(
        lags[None] >= 0, jnp.exp(-decay_rate[:, None, None] * jnp.maximum(lags, 0.0)[None]), 0.0
    )
    query_scale = jnp.exp(-decay_rate[:, None] * places[None, :]).T
    key_scale = jnp.exp(-decay_rate[:, None] * (count - places)[None, :]).T
    local = jnp.einsum(
        "shd,she->hde",
        k_blk.astype(jnp.float32) * key_scale[:, :, None],
        v_blk.astype(jnp.float32),
        precision=lax.Precision.HIGHEST,
    ).astype(jnp.bfloat16)
    states = ring_gather(local.reshape(4, heads * width // 4, width), 0)
    states = states.reshape(ring, heads, width, width).astype(jnp.float32)
    between = index - 1 - jnp.arange(ring)
    fade = jnp.where(
        between[:, None] >= 0,
        jnp.exp(
            -decay_rate[None, :] * count * jnp.maximum(between, 0)[:, None].astype(jnp.float32)
        ),
        0.0,
    )
    earlier_state = jnp.sum(fade[:, :, None, None] * states, axis=0)
    scores = jnp.einsum("thd,shd->hts", q_blk, k_blk, preferred_element_type=jnp.float32)
    weight = (scores * inside).astype(jnp.bfloat16)
    intra = jnp.einsum("hts,shd->thd", weight, v_blk, preferred_element_type=jnp.float32)
    inter = (
        jnp.einsum(
            "thd,hde->the",
            q_blk.astype(jnp.float32),
            earlier_state,
            precision=lax.Precision.HIGHEST,
        )
        * query_scale[:, :, None]
    )
    attn = rms_norm(intra + inter, -1).astype(jnp.bfloat16).reshape(4, count // 4, heads * width)
    all_heads = ring_gather(attn, 1).reshape(ring * count, heads * width)

    holders = lax.axis_size("exp")
    experts = holders // 2
    own_rows, slice_width = residual.shape
    partial = jnp.dot(all_heads, out_proj, preferred_element_type=jnp.float32).astype(jnp.bfloat16)
    parts = exchange(partial.reshape(holders, own_rows, slice_width), 2)
    summed = jnp.sum(parts.astype(jnp.float32), axis=0)
    stream = (summed + residual.astype(jnp.float32)).astype(jnp.bfloat16)

    tops = routes.shape[1]
    capacity = 2 * own_rows * tops // experts
    flat = routes.reshape(-1)
    marks = (flat[:, None] == jnp.arange(experts, dtype=jnp.int32)[None, :]).astype(jnp.int32)
    before = jnp.cumsum(marks, axis=0) - marks
    slot = jnp.sum(marks * before, axis=1)
    target = flat * capacity + slot
    placed = (target[:, None] == jnp.arange(experts * capacity, dtype=jnp.int32)[None, :]).reshape(
        own_rows, tops, experts * capacity
    )
    picker = jnp.any(placed, axis=1).astype(jnp.bfloat16)
    shares = gate_shares.astype(jnp.float32)
    shares = shares / jnp.sum(shares, axis=1, keepdims=True)
    combiner = jnp.sum(placed.astype(jnp.float32) * shares[:, :, None], axis=1)

    outgoing = lax.dot_general(
        picker, stream, (((0,), (0,)), ((), ())), preferred_element_type=jnp.float32
    ).astype(jnp.bfloat16)
    arrived = exchange(outgoing.reshape(experts, capacity, slice_width), 3)
    slots = holders * capacity
    turned = arrived.reshape(slots, slice_width).T.reshape(2, 2, slice_width // 4, slots)
    tokens = ring_gather(turned, 4, paired=True).reshape(ring * slice_width, slots)
    normed = rms_norm(tokens.astype(jnp.float32), 0).astype(jnp.bfloat16)
    gate = jnp.dot(gate_proj[0], normed, preferred_element_type=jnp.float32)
    upper = jnp.dot(up_proj[0], normed, preferred_element_type=jnp.float32)
    hidden = (jax.nn.silu(gate) * upper).astype(jnp.bfloat16)
    units = hidden.shape[0]
    whole = ring_gather(hidden.reshape(4, units // 4, slots), 5).reshape(ring * units, slots)
    produced = lax.dot_general(
        whole, down_proj[0], (((0,), (1,)), ((), ())), preferred_element_type=jnp.float32
    ).astype(jnp.bfloat16)
    homecoming = exchange(produced.reshape(holders, capacity, slice_width), 6)
    halves = homecoming.astype(jnp.float32).reshape(experts, 2, capacity, slice_width)
    expert_out = (
        (halves[:, 0] + halves[:, 1]).astype(jnp.bfloat16).reshape(experts * capacity, slice_width)
    )
    mixed = jnp.dot(combiner, expert_out.astype(jnp.float32), precision=lax.Precision.HIGHEST)
    return (stream.astype(jnp.float32) + mixed).astype(jnp.bfloat16)


def solution(mesh):
    in_specs = (
        P("ctx", "exp"),
        P("ctx", "exp"),
        P("ctx", "exp"),
        P("exp"),
        P("exp", "ctx"),
        P("exp", "ctx"),
        P("exp", None),
        P("exp", None),
        P("exp", "ctx", None),
        P("exp", "ctx", None),
        P("exp", "ctx", None),
    )
    out_specs = P("exp", "ctx")
    return jax.shard_map(body, mesh=mesh, in_specs=in_specs, out_specs=out_specs, check_vma=False)
```

```python
import functools
import jax
import jax.numpy as jnp
from jax import lax
from jax.experimental import pallas as pl
from jax.experimental.pallas import tpu as pltpu
from jax.sharding import PartitionSpec as P

MESH = pl.DeviceIdType.MESH
F32 = jnp.float32
BF16 = jnp.bfloat16
BEST = lax.Precision.HIGHEST
LANES = 128


def dot_nt(a, b):
    return lax.dot_general(a, b, (((1,), (1,)), ((), ())), preferred_element_type=F32)


def dot_nn(a, b):
    return jnp.dot(a, b, preferred_element_type=F32)


def unit(rows, cols):
    down = lax.broadcasted_iota(jnp.int32, (rows, cols), 0)
    along = lax.broadcasted_iota(jnp.int32, (rows, cols), 1)
    return (down == along).astype(F32).astype(BF16)


def layer_kernel(
    n,
    q_ref,
    k_ref,
    v_ref,
    rate_ref,
    res_ref,
    proj_ref,
    routes_ref,
    shares_ref,
    gate_hbm,
    up_hbm,
    down_hbm,
    out_ref,
    states,
    attns,
    give,
    mine,
    got,
    passed,
    land,
    res_both,
    routes_both,
    shares_both,
    turned_stream,
    leaving,
    arrived,
    tokens,
    hidden,
    product,
    half_give,
    half_got,
    turned_out,
    back,
    home,
    last,
    w_gate,
    w_up,
    w_down,
    s_send,
    s_recv,
    a_send,
    a_recv,
    t_send,
    t_recv,
    h_send,
    h_recv,
    x_send,
    x_recv,
    pair_send,
    pair_recv,
    sum_send,
    sum_recv,
    go_send,
    go_recv,
    back_send,
    back_recv,
    few_send,
    few_recv,
    w_sem,
):
    me = lax.axis_index("ctx")
    col = lax.axis_index("exp")
    chip = col // 2
    core = lax.rem(col, 2)
    partner = col + 1 - 2 * core
    half = n // 2
    near = (lax.rem(me + 1, n), lax.rem(me + n - 1, n))
    count, wide = q_ref.shape
    heads = rate_ref.shape[0]
    width = wide // heads
    own_rows, slice_width = res_ref.shape
    part_width = slice_width // 2
    slots = hidden.shape[-1]
    capacity = leaving.shape[2]
    lanes_out = n * capacity

    def remote(src, dst, send_sem, recv_sem, **where):
        return pltpu.make_async_remote_copy(
            src_ref=src,
            dst_ref=dst,
            send_sem=send_sem,
            recv_sem=recv_sem,
            device_id=where,
            device_id_type=MESH,
        )

    weights = [
        pltpu.make_async_copy(src.at[0], dst, w_sem.at[i])
        for i, (src, dst) in enumerate(((gate_hbm, w_gate), (up_hbm, w_up), (down_hbm, w_down)))
    ]
    for copy in weights:
        copy.start()

    barrier = pltpu.get_barrier_semaphore()
    for peer in near:
        pl.semaphore_signal(barrier, inc=1, device_id={"ctx": peer}, device_id_type=MESH)
    pl.semaphore_signal(barrier, inc=1, device_id={"exp": partner}, device_id_type=MESH)

    def greet(j, carry):
        peer = 2 * lax.rem(chip + j, n) + core
        pl.semaphore_signal(barrier, inc=1, device_id={"exp": peer}, device_id_type=MESH)
        return carry

    lax.fori_loop(1, n, greet, 0)

    down_iota = lax.broadcasted_iota(jnp.int32, (count, width), 0).astype(F32)
    along_iota = lax.broadcasted_iota(jnp.int32, (count, width), 1).astype(F32)
    head_at = [slice(h * width, (h + 1) * width) for h in range(heads)]
    for h in range(heads):
        faded = k_ref[:, head_at[h]].astype(F32) * jnp.exp(-rate_ref[h] * (count - down_iota))
        local = jnp.dot(
            faded.T, v_ref[:, head_at[h]].astype(F32), precision=BEST, preferred_element_type=F32
        ).astype(BF16)
        states[me, 2 * h] = local[: width // 2]
        states[me, 2 * h + 1] = local[width // 2 :]
    res_both[pl.ds(pl.multiple_of(core * own_rows, own_rows), own_rows), :] = res_ref[...]
    routes_both[core] = routes_ref[...]
    shares_both[core] = shares_ref[...]
    pl.semaphore_wait(barrier, n + 2)

    rows_mine = res_both.at[pl.ds(pl.multiple_of(core * own_rows, own_rows), own_rows), :]
    rows_other = res_both.at[pl.ds(pl.multiple_of((1 - core) * own_rows, own_rows), own_rows), :]
    early = [
        (remote(res_ref, rows_mine, few_send.at[0], few_recv.at[0], exp=partner), rows_other),
        (
            remote(routes_ref, routes_both.at[core], few_send.at[1], few_recv.at[1], exp=partner),
            routes_both.at[1 - core],
        ),
        (
            remote(shares_ref, shares_both.at[core], few_send.at[2], few_recv.at[2], exp=partner),
            shares_both.at[1 - core],
        ),
    ]

    def origin_of(way, step):
        return lax.rem(me - step + n, n) if way == 0 else lax.rem(me + step, n)

    def ring(place, chunks, send, recv, work, forward=None):
        def hop(way, step, chunk):
            spot = place(origin_of(way, step), chunk)
            sems = (send.at[way, step, chunk], recv.at[way, step, chunk])
            return remote(spot, spot, *sems, ctx=near[way])

        def landed(way, step, chunk):
            spot = place(origin_of(way, step + 1), chunk)
            sems = (send.at[way, step, chunk], recv.at[way, step, chunk])
            return remote(spot, spot, *sems, ctx=near[way])

        def ends(way, chunk):
            return (chunk < chunks // 2) == (way == 0)

        every = [(chunk, way) for chunk in range(chunks) for way in range(2)]
        last_hop = [(chunk, way) for chunk, way in every if ends(way, chunk)]

        def turn(step, arriving, going):
            for chunk, way in every:
                if (chunk, way) in arriving:
                    landed(way, step - 1, chunk).wait_recv()
                if (chunk, way) in going:
                    hop(way, step, chunk).start()
                if forward is not None and (chunk, way) in arriving:
                    forward(way, step - 1, chunk).start()

        turn(0, [], every)
        work(0, [me])
        turn(1, every, every)
        work(1, [origin_of(0, 1), origin_of(1, 1)])

        def middle(step, carry):
            turn(step, every, every)
            work(step, [origin_of(0, step), origin_of(1, step)])
            return carry

        lax.fori_loop(2, half - 1, middle, 0)
        turn(half - 1, every, last_hop)
        work(half - 1, [origin_of(0, half - 1), origin_of(1, half - 1)])
        turn(half, last_hop, [])
        work(half, [origin_of(0, half)])

        def drain():
            def sent(step, carry):
                for chunk, way in every:
                    hop(way, step, chunk).wait_send()
                return carry

            lax.fori_loop(0, half - 1, sent, 0)
            for chunk, way in last_hop:
                hop(way, half - 1, chunk).wait_send()

        return drain

    lags = down_iota - along_iota
    inner = []

    def inside(step, origins):
        if isinstance(step, int) and step == 0:
            for copy, _ in early:
                copy.start()
            for h in range(heads):
                scores = dot_nt(q_ref[:, head_at[h]], k_ref[:, head_at[h]])
                keep = jnp.where(lags >= 0, jnp.exp(-rate_ref[h] * jnp.maximum(lags, 0.0)), 0.0)
                inner.append(dot_nn((scores * keep).astype(BF16), v_ref[:, head_at[h]]))

    drains = [ring(lambda o, c: states.at[o, c], states.shape[1], s_send, s_recv, inside)]
    for h in range(heads):

        def add_state(j, total, h=h):
            between = me - 1 - j
            span = jnp.full((1, width), jnp.maximum(between, 0)).astype(F32)
            fade = jnp.where(between >= 0, jnp.exp(-rate_ref[h] * count * span), 0.0)
            return total + fade * states[j, pl.ds(2 * h, 2)].reshape(width, width).astype(F32)

        earlier = lax.fori_loop(0, n, add_state, jnp.zeros((width, width), F32))
        across = jnp.dot(
            q_ref[:, head_at[h]].astype(F32), earlier, precision=BEST, preferred_element_type=F32
        )
        mixed = inner[h] + across * jnp.exp(-rate_ref[h] * down_iota)
        scale = lax.rsqrt(jnp.mean(mixed * mixed, axis=-1, keepdims=True) + 1e-06)
        attn = (mixed * scale).astype(BF16)
        piece = count // attns.shape[1]
        for c in range(attns.shape[1]):
            attns[me, c, :, head_at[h]] = attn[c * piece : (c + 1) * piece]

    def pair_copy(o):
        return remote(give.at[o], got.at[o], pair_send.at[o], pair_recv.at[o], exp=partner)

    def sum_copy(o):
        sems = (sum_send.at[o], sum_recv.at[chip])
        return remote(passed.at[o], land.at[chip], *sems, exp=2 * o + core)

    def split(value):
        low, high = value[:part_width], value[part_width:]
        return jnp.where(core == 0, low, high), jnp.where(core == 0, high, low)

    def project(o):
        block = attns[o].reshape(count, wide)
        kept, given = split(dot_nt(proj_ref[...], block))
        mine[o] = kept
        give[o] = given.astype(BF16)
        pair_copy(o).start()

    def hand_on(o):
        pair_copy(o).wait_recv()
        total = (mine[o] + got[o].astype(F32)).astype(BF16)

        @pl.when(o == chip)
        def _():
            land[o] = total

        @pl.when(o != chip)
        def _():
            passed[o] = total
            sum_copy(o).start()

    def out_step(step, origins):
        for o in origins:
            project(o)
        if isinstance(step, int) and step == 1:
            hand_on(me)
        elif not (isinstance(step, int) and step == 0):
            hand_on(origin_of(0, step - 1))
            hand_on(origin_of(1, step - 1))
        if isinstance(step, int) and step == half:
            hand_on(origin_of(0, half))

    drains.append(ring(lambda o, c: attns.at[o, c], attns.shape[1], a_send, a_recv, out_step))

    for copy, spot in early:
        copy.wait_send()
    for i, (copy, spot) in enumerate(early):
        remote(spot, spot, few_send.at[i], few_recv.at[i], exp=partner).wait_recv()

    lane = lax.broadcasted_iota(jnp.int32, (own_rows, lanes_out), 1)
    expert_of, slot_of = lane // capacity, lax.rem(lane, capacity)
    before = (
        lax.broadcasted_iota(jnp.int32, (own_rows, own_rows), 0)
        > lax.broadcasted_iota(jnp.int32, (own_rows, own_rows), 1)
    ).astype(F32)
    flip = unit(lanes_out, lanes_out)
    pickers, combiners = [], []
    for b in range(2):
        first = (routes_both[b, :, 0:1] == expert_of).astype(F32)
        second = (routes_both[b, :, 1:2] == expert_of).astype(F32)
        named = first + second
        rank = dot_nn(before.astype(BF16), named.astype(BF16))
        placed = jnp.where(rank == slot_of.astype(F32), named, 0.0)
        part = shares_both[b].astype(F32)
        whole = part[:, 0:1] + part[:, 1:2]
        combiners.append(placed * (first * (part[:, 0:1] / whole) + second * (part[:, 1:2] / whole)))
        pickers.append(dot_nt(flip, placed.astype(BF16)).astype(BF16))

    choose = (
        lax.broadcasted_iota(jnp.int32, (part_width, slice_width), 0) + core * part_width
        == lax.broadcasted_iota(jnp.int32, (part_width, slice_width), 1)
    ).astype(F32)
    start = dot_nt(choose.astype(BF16), res_both[...])

    def sum_landed(p):
        sems = (sum_send.at[p], sum_recv.at[p])
        return remote(land.at[p], land.at[p], *sems, exp=2 * p + core)

    def add_part(j, total):
        p = lax.rem(chip + j, n)

        @pl.when(j > 0)
        def _():
            sum_landed(p).wait_recv()

        return total + land[p].astype(F32)

    stream = lax.fori_loop(0, n, add_part, jnp.zeros((part_width, count), F32))
    stream = (stream + start).astype(BF16)
    turned_stream[pl.ds(part_width, LANES - part_width), :] = jnp.zeros(
        (LANES - part_width, count), BF16
    )
    turned_stream[pl.ds(0, part_width), :] = stream
    by_token = dot_nt(unit(count, count), turned_stream[...]).astype(BF16)
    by_block = [by_token[:own_rows], by_token[own_rows:]]

    def exchange(src, dst, send, recv):
        def outward(j):
            p = lax.rem(chip + j, n)
            return remote(src.at[p], dst.at[chip], send.at[p], recv.at[chip], exp=2 * p + core)

        def inward(j):
            p = lax.rem(chip + j, n)
            return remote(dst.at[p], dst.at[p], send.at[p], recv.at[p], exp=2 * p + core)

        def launch(j, carry):
            outward(j).start()
            return carry

        def finish(j, carry):
            inward(j).wait_recv()
            return carry

        def sent(j, carry):
            outward(j).wait_send()
            return carry

        lax.fori_loop(1, n, launch, 0)
        dst[chip] = src[chip]
        lax.fori_loop(1, n, finish, 0)
        drains.append(lambda: lax.fori_loop(1, n, sent, 0))

    for b in range(2):
        picked = dot_nn(pickers[b], by_block[b]).astype(BF16)
        leaving[:, b] = picked.reshape(n, capacity, LANES)
    exchange(leaving, arrived, go_send, go_recv)

    turned = dot_nt(unit(part_width, LANES), arrived[...].reshape(slots, LANES)).astype(BF16)
    chunks = tokens.shape[2]
    piece = part_width // chunks
    for c in range(chunks):
        tokens[me, core, c] = turned[c * piece : (c + 1) * piece]

    def hand_across(way, step, chunk):
        spot = tokens.at[origin_of(way, step + 1), core, chunk]
        sems = (x_send.at[way, step, chunk], x_recv.at[way, step, chunk])
        return remote(spot, spot, *sems, exp=partner)

    def handed(way, step, chunk):
        spot = tokens.at[origin_of(way, step + 1), 1 - core, chunk]
        sems = (x_send.at[way, step, chunk], x_recv.at[way, step, chunk])
        return remote(spot, spot, *sems, exp=partner)

    def own_across(side):
        spot = tokens.at[me, side]
        return remote(spot, spot, few_send.at[3], few_recv.at[3], exp=partner)

    def start_own(step, origins):
        if isinstance(step, int) and step == 0:
            own_across(core).start()

    drains.append(
        ring(lambda o, c: tokens.at[o, core, c], chunks, t_send, t_recv, start_own, hand_across)
    )
    own_across(1 - core).wait_recv()
    ways = [(chunk, way) for chunk in range(chunks) for way in range(2)]

    def all_handed(step, carry):
        for chunk, way in ways:
            handed(way, step, chunk).wait_recv()
        return carry

    lax.fori_loop(0, half - 1, all_handed, 0)
    ending = [(chunk, way) for chunk, way in ways if (chunk < chunks // 2) == (way == 0)]
    for chunk, way in ending:
        handed(way, half - 1, chunk).wait_recv()

    def across_sent():
        def sent(step, carry):
            for chunk, way in ways:
                hand_across(way, step, chunk).wait_send()
            return carry

        lax.fori_loop(0, half - 1, sent, 0)
        for chunk, way in ending:
            hand_across(way, half - 1, chunk).wait_send()
        own_across(core).wait_send()

    drains.append(across_sent)

    for copy in weights:
        copy.wait()
    group = 4
    gate = upper = square = 0.0
    for i in range(n // group):
        block = tokens[pl.ds(i * group, group)].reshape(group * slice_width, slots)
        span = slice(i * group * slice_width, (i + 1) * group * slice_width)
        gate += dot_nn(w_gate[:, span], block)
        upper += dot_nn(w_up[:, span], block)
        wide_block = block.astype(F32)
        square += jnp.sum(wide_block * wide_block, axis=0, keepdims=True)
    scale = lax.rsqrt(square / (n * slice_width) + 1e-06)
    gate = gate * scale
    unit_rows = (gate / (1.0 + jnp.exp(-gate)) * (upper * scale)).astype(BF16)
    units = unit_rows.shape[0]
    piece = units // hidden.shape[1]
    for c in range(hidden.shape[1]):
        hidden[me, c] = unit_rows[c * piece : (c + 1) * piece]

    def down_step(step, origins):
        for o in origins:
            at = pl.ds(pl.multiple_of(o * units, units), units)
            term = dot_nn(w_down[:, at], hidden[o].reshape(units, slots))
            if isinstance(step, int) and step == 0:
                product[...] = term
            else:
                product[...] += term

    drains.append(ring(lambda o, c: hidden.at[o, c], hidden.shape[1], h_send, h_recv, down_step))

    kept, given = split(product[...])
    half_give[...] = given.astype(BF16)
    swap = remote(half_give, half_got, few_send.at[4], few_recv.at[4], exp=partner)
    swap.start()
    swap.wait_recv()
    turned_out[pl.ds(part_width, LANES - part_width), :] = jnp.zeros(
        (LANES - part_width, slots), BF16
    )
    turned_out[pl.ds(0, part_width), :] = (kept + half_got[...].astype(F32)).astype(BF16)
    owners = LANES // (2 * capacity)
    for j in range(slots // LANES):
        rows = dot_nt(unit(LANES, LANES), turned_out[:, j * LANES : (j + 1) * LANES])
        back[pl.ds(j * owners, owners)] = rows.astype(BF16).reshape(owners, 2, capacity, LANES)
    exchange(back, home, back_send, back_recv)

    final = []
    for b in range(2):
        outs = home[:, b].reshape(lanes_out, LANES).astype(F32)
        mixed = jnp.dot(combiners[b], outs, precision=BEST, preferred_element_type=F32)
        final.append(by_block[b].astype(F32) + mixed)
    last[...] = jnp.where(core == 0, final[1], final[0]).astype(BF16)
    swap_last = remote(last, out_ref.at[core], few_send.at[5], few_recv.at[5], exp=partner)
    swap_last.start()
    out_ref[core] = jnp.where(core == 0, final[0], final[1]).astype(BF16)

    for drain in drains:
        drain()

    def pairs_sent(o, carry):
        pair_copy(o).wait_send()
        return carry

    lax.fori_loop(0, n, pairs_sent, 0)

    def sums_sent(j, carry):
        sum_copy(lax.rem(chip + j, n)).wait_send()
        return carry

    lax.fori_loop(1, n, sums_sent, 0)
    swap.wait_send()
    swap_last.wait_send()
    spot = out_ref.at[1 - core]
    remote(spot, spot, few_send.at[5], few_recv.at[5], exp=partner).wait_recv()


def body(
    queries,
    key_rows,
    value_rows,
    decay_rate,
    residual,
    out_proj,
    routes,
    gate_shares,
    gate_proj,
    up_proj,
    down_proj,
):
    n = lax.axis_size("ctx")
    holders = lax.axis_size("exp")
    count, wide = queries.shape
    heads = decay_rate.shape[0]
    width = wide // heads
    own_rows, slice_width = residual.shape
    part_width = slice_width // 2
    capacity = 2 * own_rows * routes.shape[1] // n
    slots = holders * capacity
    units = gate_proj.shape[1]
    vmem, dma = pltpu.VMEM, pltpu.SemaphoreType.DMA
    on_chip = pl.BlockSpec(memory_space=pltpu.VMEM)
    anywhere = pl.BlockSpec(memory_space=pl.ANY)
    half = n // 2
    ring4, ring2, each = dma((2, half, 4)), dma((2, half, 2)), dma((n,))
    out = pl.pallas_call(
        functools.partial(layer_kernel, n),
        out_shape=jax.ShapeDtypeStruct((2, own_rows, LANES), BF16),
        in_specs=[on_chip] * 3
        + [pl.BlockSpec(memory_space=pltpu.SMEM)]
        + [on_chip] * 4
        + [anywhere] * 3,
        out_specs=on_chip,
        scratch_shapes=[
            vmem((n, 2 * heads, width // 2, width), BF16),
            vmem((n, 4, count // 4, wide), BF16),
            vmem((n, part_width, count), BF16),
            vmem((n, part_width, count), F32),
            vmem((n, part_width, count), BF16),
            vmem((n, part_width, count), BF16),
            vmem((n, part_width, count), BF16),
            vmem((2 * own_rows, slice_width), BF16),
            vmem((2,) + routes.shape, jnp.int32),
            vmem((2,) + routes.shape, jnp.int32),
            vmem((LANES, count), BF16),
            vmem((n, 2, capacity, LANES), BF16),
            vmem((n, 2, capacity, LANES), BF16),
            vmem((n, 2, 2, part_width // 2, slots), BF16),
            vmem((n, 4, units // 4, slots), BF16),
            vmem((slice_width, slots), F32),
            vmem((part_width, slots), BF16),
            vmem((part_width, slots), BF16),
            vmem((LANES, slots), BF16),
            vmem((n, 2, capacity, LANES), BF16),
            vmem((n, 2, capacity, LANES), BF16),
            vmem((own_rows, LANES), BF16),
            vmem(gate_proj.shape[1:], BF16),
            vmem(up_proj.shape[1:], BF16),
            vmem(down_proj.shape[1:], BF16),
        ]
        + [ring4] * 4
        + [ring2] * 2
        + [ring4] * 2
        + [ring2] * 2
        + [each] * 8
        + [dma((6,))] * 2
        + [dma((3,))],
        compiler_params=pltpu.CompilerParams(
            collective_id=0, has_side_effects=True, vmem_limit_bytes=56 * 2**20
        ),
        name="layer",
    )(
        queries,
        key_rows,
        value_rows,
        decay_rate,
        residual,
        out_proj.T,
        routes,
        gate_shares,
        gate_proj,
        up_proj,
        down_proj,
    )
    return jnp.concatenate([out[0, :, :part_width], out[1, :, :part_width]], axis=1)


def solution(mesh):
    in_specs = (
        P("ctx", "exp"),
        P("ctx", "exp"),
        P("ctx", "exp"),
        P("exp"),
        P("exp", "ctx"),
        P("exp", "ctx"),
        P("exp", None),
        P("exp", None),
        P("exp", "ctx", None),
        P("exp", "ctx", None),
        P("exp", "ctx", None),
    )
    out_specs = P("exp", "ctx")
    return jax.shard_map(body, mesh=mesh, in_specs=in_specs, out_specs=out_specs, check_vma=False)
```

```python
import functools
import jax
import jax.numpy as jnp
from jax import lax
from jax.experimental import pallas as pl
from jax.experimental.pallas import tpu as pltpu
from jax.sharding import PartitionSpec as P

MESH = pl.DeviceIdType.MESH
F32 = jnp.float32
BF16 = jnp.bfloat16
BEST = lax.Precision.HIGHEST
LANES = 128


def dot_nt(a, b):
    return lax.dot_general(a, b, (((1,), (1,)), ((), ())), preferred_element_type=F32)


def dot_nn(a, b):
    return jnp.dot(a, b, preferred_element_type=F32)


def unit(rows, cols):
    down = lax.broadcasted_iota(jnp.int32, (rows, cols), 0)
    along = lax.broadcasted_iota(jnp.int32, (rows, cols), 1)
    return (down == along).astype(F32).astype(BF16)


def layer_kernel(
    n,
    q_ref,
    k_ref,
    v_ref,
    rate_ref,
    res_ref,
    proj_ref,
    routes_ref,
    shares_ref,
    gate_hbm,
    up_hbm,
    down_hbm,
    out_ref,
    states,
    attns,
    give,
    mine,
    got,
    passed,
    land,
    res_both,
    routes_both,
    shares_both,
    turned_stream,
    leaving,
    arrived,
    tokens,
    hidden,
    product,
    half_give,
    half_got,
    turned_out,
    back,
    home,
    last,
    w_gate,
    w_up,
    w_down,
    gate_sum,
    up_sum,
    square,
    s_send,
    s_recv,
    a_send,
    a_recv,
    t_send,
    t_recv,
    h_send,
    h_recv,
    x_send,
    x_recv,
    pair_send,
    pair_recv,
    sum_send,
    sum_recv,
    go_send,
    go_recv,
    back_send,
    back_recv,
    few_send,
    few_recv,
    w_sem,
):
    me = lax.axis_index("ctx")
    col = lax.axis_index("exp")
    chip = col // 2
    core = lax.rem(col, 2)
    partner = col + 1 - 2 * core
    half = n // 2

    def along(way, steps):
        return lax.rem(me + steps, n) if way == 0 else lax.rem(me - steps + n, n)

    count, wide = q_ref.shape
    heads = rate_ref.shape[0]
    width = wide // heads
    own_rows, slice_width = res_ref.shape
    part_width = slice_width // 2
    slots = hidden.shape[-1]
    capacity = leaving.shape[2]
    lanes_out = n * capacity

    def remote(src, dst, send_sem, recv_sem, **where):
        return pltpu.make_async_remote_copy(
            src_ref=src,
            dst_ref=dst,
            send_sem=send_sem,
            recv_sem=recv_sem,
            device_id=where,
            device_id_type=MESH,
        )

    weights = [
        pltpu.make_async_copy(src.at[0], dst, w_sem.at[i])
        for i, (src, dst) in enumerate(((gate_hbm, w_gate), (up_hbm, w_up), (down_hbm, w_down)))
    ]
    for copy in weights:
        copy.start()

    barrier = pltpu.get_barrier_semaphore()
    for steps in (1, 2):
        for way in range(2):
            peer = along(way, steps)
            pl.semaphore_signal(barrier, inc=1, device_id={"ctx": peer}, device_id_type=MESH)
    pl.semaphore_signal(barrier, inc=1, device_id={"exp": partner}, device_id_type=MESH)

    def greet(j, carry):
        peer = 2 * lax.rem(chip + j, n) + core
        pl.semaphore_signal(barrier, inc=1, device_id={"exp": peer}, device_id_type=MESH)
        return carry

    lax.fori_loop(1, n, greet, 0)

    down_iota = lax.broadcasted_iota(jnp.int32, (count, width), 0).astype(F32)
    right_iota = lax.broadcasted_iota(jnp.int32, (count, width), 1).astype(F32)
    head_at = [slice(h * width, (h + 1) * width) for h in range(heads)]
    for h in range(heads):
        faded = k_ref[:, head_at[h]].astype(F32) * jnp.exp(-rate_ref[h] * (count - down_iota))
        local = jnp.dot(
            faded.T, v_ref[:, head_at[h]].astype(F32), precision=BEST, preferred_element_type=F32
        ).astype(BF16)
        states[me, 2 * h] = local[: width // 2]
        states[me, 2 * h + 1] = local[width // 2 :]
    res_both[pl.ds(pl.multiple_of(core * own_rows, own_rows), own_rows), :] = res_ref[...]
    routes_both[core] = routes_ref[...]
    shares_both[core] = shares_ref[...]
    pl.semaphore_wait(barrier, n + 4)

    rows_mine = res_both.at[pl.ds(pl.multiple_of(core * own_rows, own_rows), own_rows), :]
    rows_other = res_both.at[pl.ds(pl.multiple_of((1 - core) * own_rows, own_rows), own_rows), :]
    early = [
        (remote(res_ref, rows_mine, few_send.at[0], few_recv.at[0], exp=partner), rows_other),
        (
            remote(routes_ref, routes_both.at[core], few_send.at[1], few_recv.at[1], exp=partner),
            routes_both.at[1 - core],
        ),
        (
            remote(shares_ref, shares_both.at[core], few_send.at[2], few_recv.at[2], exp=partner),
            shares_both.at[1 - core],
        ),
    ]

    def origin_of(way, step):
        return along(1 - way, step)

    def ring(place, chunks, send, recv, work, forward=None, skip=False):
        def hop(way, step, stride, chunk):
            spot = place(origin_of(way, step - stride), chunk)
            sems = (send.at[way, step - 1, chunk], recv.at[way, step - 1, chunk])
            return remote(spot, spot, *sems, ctx=along(way, stride))

        def landed(way, step, chunk):
            spot = place(origin_of(way, step), chunk)
            sems = (send.at[way, step - 1, chunk], recv.at[way, step - 1, chunk])
            return remote(spot, spot, *sems, ctx=along(way, 1))

        every = [(chunk, way) for chunk in range(chunks) for way in range(2)]
        last_hop = [(chunk, way) for chunk, way in every if (chunk < chunks // 2) == (way == 0)]

        def turn(step, even, arriving, far, close):
            for chunk, way in every:
                if (chunk, way) in arriving:
                    landed(way, step, chunk).wait_recv()
                if skip and even and (chunk, way) in far:
                    hop(way, step + 2, 2, chunk).start()
                if (not skip or even) and (chunk, way) in close:
                    hop(way, step + 1, 1, chunk).start()
                if forward is not None and (chunk, way) in arriving:
                    forward(way, step, chunk).start()

        def both(step):
            return [origin_of(0, step), origin_of(1, step)]

        turn(0, True, [], every, every)
        work(0, [me])
        turn(1, False, every, every, every)
        work(1, both(1))

        def middle(i, carry):
            turn(2 * i, True, every, every, every)
            work(2 * i, both(2 * i))
            turn(2 * i + 1, False, every, every, every)
            work(2 * i + 1, both(2 * i + 1))
            return carry

        lax.fori_loop(1, half // 2 - 1, middle, 0)
        turn(half - 2, True, every, last_hop, every)
        work(half - 2, both(half - 2))
        turn(half - 1, False, every, [], last_hop)
        work(half - 1, both(half - 1))
        turn(half, True, last_hop, [], [])
        work(half, [origin_of(0, half)])

        def drain():
            def sent(step, carry):
                for chunk, way in every:
                    landed(way, step, chunk).wait_send()
                return carry

            lax.fori_loop(1, half, sent, 0)
            for chunk, way in last_hop:
                landed(way, half, chunk).wait_send()

        return drain

    lags = down_iota - right_iota
    inner = []

    def inside(step, origins):
        if isinstance(step, int) and step == 0:
            for copy, _ in early:
                copy.start()
            for h in range(heads):
                scores = dot_nt(q_ref[:, head_at[h]], k_ref[:, head_at[h]])
                keep = jnp.where(lags >= 0, jnp.exp(-rate_ref[h] * jnp.maximum(lags, 0.0)), 0.0)
                inner.append(dot_nn((scores * keep).astype(BF16), v_ref[:, head_at[h]]))

    drains = [
        ring(lambda o, c: states.at[o, c], states.shape[1], s_send, s_recv, inside, skip=True)
    ]
    for h in range(heads):

        def add_state(j, total, h=h):
            between = me - 1 - j
            span = jnp.full((1, width), jnp.maximum(between, 0)).astype(F32)
            fade = jnp.where(between >= 0, jnp.exp(-rate_ref[h] * count * span), 0.0)
            return total + fade * states[j, pl.ds(2 * h, 2)].reshape(width, width).astype(F32)

        earlier = lax.fori_loop(0, n, add_state, jnp.zeros((width, width), F32))
        across = jnp.dot(
            q_ref[:, head_at[h]].astype(F32), earlier, precision=BEST, preferred_element_type=F32
        )
        mixed = inner[h] + across * jnp.exp(-rate_ref[h] * down_iota)
        scale = lax.rsqrt(jnp.mean(mixed * mixed, axis=-1, keepdims=True) + 1e-06)
        attn = (mixed * scale).astype(BF16)
        piece = count // attns.shape[1]
        for c in range(attns.shape[1]):
            attns[me, c, :, head_at[h]] = attn[c * piece : (c + 1) * piece]

    def pair_copy(o):
        return remote(give.at[o], got.at[o], pair_send.at[o], pair_recv.at[o], exp=partner)

    def sum_copy(o):
        sems = (sum_send.at[o], sum_recv.at[chip])
        return remote(passed.at[o], land.at[chip], *sems, exp=2 * o + core)

    def split(value):
        low, high = value[:part_width], value[part_width:]
        return jnp.where(core == 0, low, high), jnp.where(core == 0, high, low)

    def project(o):
        block = attns[o].reshape(count, wide)
        kept, given = split(dot_nt(proj_ref[...], block))
        mine[o] = kept
        give[o] = given.astype(BF16)
        pair_copy(o).start()

    def hand_on(o):
        pair_copy(o).wait_recv()
        total = (mine[o] + got[o].astype(F32)).astype(BF16)

        @pl.when(o == chip)
        def _():
            land[o] = total

        @pl.when(o != chip)
        def _():
            passed[o] = total
            sum_copy(o).start()

    def out_step(step, origins):
        for o in origins:
            project(o)
        if isinstance(step, int) and step == 1:
            hand_on(me)
        elif not (isinstance(step, int) and step == 0):
            hand_on(origin_of(0, step - 1))
            hand_on(origin_of(1, step - 1))
        if isinstance(step, int) and step == half:
            hand_on(origin_of(0, half))

    drains.append(
        ring(lambda o, c: attns.at[o, c], attns.shape[1], a_send, a_recv, out_step, skip=True)
    )

    for copy, spot in early:
        copy.wait_send()
    for i, (copy, spot) in enumerate(early):
        remote(spot, spot, few_send.at[i], few_recv.at[i], exp=partner).wait_recv()

    lane = lax.broadcasted_iota(jnp.int32, (own_rows, lanes_out), 1)
    expert_of, slot_of = (lane // capacity).astype(F32), lax.rem(lane, capacity).astype(F32)
    upright = unit(own_rows, own_rows)
    before = (
        lax.broadcasted_iota(jnp.int32, (own_rows, own_rows), 0)
        > lax.broadcasted_iota(jnp.int32, (own_rows, own_rows), 1)
    ).astype(F32)
    flip = unit(lanes_out, lanes_out)
    pickers, combiners = [], []
    for b in range(2):
        chosen = dot_nt(upright, routes_both[b].astype(F32).astype(BF16))
        first = (chosen[:, 0:1] == expert_of).astype(F32)
        second = (chosen[:, 1:2] == expert_of).astype(F32)
        named = first + second
        rank = dot_nn(before.astype(BF16), named.astype(BF16))
        placed = jnp.where(rank == slot_of, named, 0.0)
        part = dot_nt(upright, shares_both[b].astype(F32).astype(BF16))
        whole = part[:, 0:1] + part[:, 1:2]
        combiners.append(placed * (first * (part[:, 0:1] / whole) + second * (part[:, 1:2] / whole)))
        pickers.append(dot_nt(flip, placed.astype(BF16)).astype(BF16))

    choose = (
        lax.broadcasted_iota(jnp.int32, (part_width, slice_width), 0) + core * part_width
        == lax.broadcasted_iota(jnp.int32, (part_width, slice_width), 1)
    ).astype(F32)
    start = dot_nt(choose.astype(BF16), res_both[...])

    def sum_landed(p):
        sems = (sum_send.at[p], sum_recv.at[p])
        return remote(land.at[p], land.at[p], *sems, exp=2 * p + core)

    def add_part(j, total):
        p = lax.rem(chip + j, n)

        @pl.when(j > 0)
        def _():
            sum_landed(p).wait_recv()

        return total + land[p].astype(F32)

    stream = lax.fori_loop(0, n, add_part, jnp.zeros((part_width, count), F32))
    stream = (stream + start).astype(BF16)
    turned_stream[pl.ds(part_width, LANES - part_width), :] = jnp.zeros(
        (LANES - part_width, count), BF16
    )
    turned_stream[pl.ds(0, part_width), :] = stream
    by_token = dot_nt(unit(count, count), turned_stream[...]).astype(BF16)
    by_block = [by_token[:own_rows], by_token[own_rows:]]

    def exchange(src, dst, send, recv):
        def outward(j):
            p = lax.rem(chip + j, n)
            return remote(src.at[p], dst.at[chip], send.at[p], recv.at[chip], exp=2 * p + core)

        def inward(j):
            p = lax.rem(chip + j, n)
            return remote(dst.at[p], dst.at[p], send.at[p], recv.at[p], exp=2 * p + core)

        def launch(j, carry):
            outward(j).start()
            return carry

        def finish(j, carry):
            inward(j).wait_recv()
            return carry

        def sent(j, carry):
            outward(j).wait_send()
            return carry

        lax.fori_loop(1, n, launch, 0)
        dst[chip] = src[chip]
        lax.fori_loop(1, n, finish, 0)
        drains.append(lambda: lax.fori_loop(1, n, sent, 0))

    for b in range(2):
        picked = dot_nn(pickers[b], by_block[b]).astype(BF16)
        leaving[:, b] = picked.reshape(n, capacity, LANES)
    exchange(leaving, arrived, go_send, go_recv)

    turned = dot_nt(unit(part_width, LANES), arrived[...].reshape(slots, LANES)).astype(BF16)
    chunks = tokens.shape[2]
    piece = part_width // chunks
    for c in range(chunks):
        tokens[me, core, c] = turned[c * piece : (c + 1) * piece]

    def hand_across(way, step, chunk):
        spot = tokens.at[origin_of(way, step), core, chunk]
        sems = (x_send.at[way, step - 1, chunk], x_recv.at[way, step - 1, chunk])
        return remote(spot, spot, *sems, exp=partner)

    def handed(way, step, chunk):
        spot = tokens.at[origin_of(way, step), 1 - core, chunk]
        sems = (x_send.at[way, step - 1, chunk], x_recv.at[way, step - 1, chunk])
        return remote(spot, spot, *sems, exp=partner)

    def own_across(side):
        spot = tokens.at[me, side]
        return remote(spot, spot, few_send.at[3], few_recv.at[3], exp=partner)

    ways = [(chunk, way) for chunk in range(chunks) for way in range(2)]
    ending = [(chunk, way) for chunk, way in ways if (chunk < chunks // 2) == (way == 0)]

    def multiply(step, arrivals):
        for chunk, way in arrivals:
            handed(way, step, chunk).wait_recv()
        odd = lax.rem(me + step, 2) == 1
        base = lax.rem(jnp.where(odd, me + step - 1, me - step + n), n)
        block = tokens[pl.ds(base, 2)].reshape(2 * slice_width, slots)
        span = pl.ds(pl.multiple_of(base * slice_width, 2 * slice_width), 2 * slice_width)
        gate_sum[...] += dot_nn(w_gate[:, span], block)
        up_sum[...] += dot_nn(w_up[:, span], block)
        wide_block = block.astype(F32)
        square[...] += jnp.sum(wide_block * wide_block, axis=0, keepdims=True)

    def token_step(step, origins):
        if isinstance(step, int) and step == 0:
            own_across(core).start()
            gate_sum[...] = jnp.zeros_like(gate_sum)
            up_sum[...] = jnp.zeros_like(up_sum)
            square[...] = jnp.zeros_like(square)
        elif isinstance(step, int) and step == 1:
            for copy in weights:
                copy.wait()
            own_across(1 - core).wait_recv()
        else:
            multiply(step - 1, ways)

    drains.append(
        ring(lambda o, c: tokens.at[o, core, c], chunks, t_send, t_recv, token_step, hand_across)
    )
    multiply(half, ending)

    def across_sent():
        def sent(step, carry):
            for chunk, way in ways:
                hand_across(way, step, chunk).wait_send()
            return carry

        lax.fori_loop(1, half, sent, 0)
        for chunk, way in ending:
            hand_across(way, half, chunk).wait_send()
        own_across(core).wait_send()

    drains.append(across_sent)

    scale = lax.rsqrt(square[...] / (n * slice_width) + 1e-06)
    gate = gate_sum[...] * scale
    upper = up_sum[...] * scale
    unit_rows = (gate / (1.0 + jnp.exp(-gate)) * upper).astype(BF16)
    units = unit_rows.shape[0]
    piece = units // hidden.shape[1]
    for c in range(hidden.shape[1]):
        hidden[me, c] = unit_rows[c * piece : (c + 1) * piece]

    def down_step(step, origins):
        for o in origins:
            at = pl.ds(pl.multiple_of(o * units, units), units)
            term = dot_nn(w_down[:, at], hidden[o].reshape(units, slots))
            if isinstance(step, int) and step == 0:
                product[...] = term
            else:
                product[...] += term

    drains.append(ring(lambda o, c: hidden.at[o, c], hidden.shape[1], h_send, h_recv, down_step))

    kept, given = split(product[...])
    half_give[...] = given.astype(BF16)
    swap = remote(half_give, half_got, few_send.at[4], few_recv.at[4], exp=partner)
    swap.start()
    swap.wait_recv()
    turned_out[pl.ds(part_width, LANES - part_width), :] = jnp.zeros(
        (LANES - part_width, slots), BF16
    )
    turned_out[pl.ds(0, part_width), :] = (kept + half_got[...].astype(F32)).astype(BF16)
    owners = LANES // (2 * capacity)
    for j in range(slots // LANES):
        rows = dot_nt(unit(LANES, LANES), turned_out[:, j * LANES : (j + 1) * LANES])
        back[pl.ds(j * owners, owners)] = rows.astype(BF16).reshape(owners, 2, capacity, LANES)
    exchange(back, home, back_send, back_recv)

    final = []
    for b in range(2):
        outs = home[:, b].reshape(lanes_out, LANES).astype(F32)
        mixed = jnp.dot(combiners[b], outs, precision=BEST, preferred_element_type=F32)
        final.append(by_block[b].astype(F32) + mixed)
    last[...] = jnp.where(core == 0, final[1], final[0]).astype(BF16)
    swap_last = remote(last, out_ref.at[core], few_send.at[5], few_recv.at[5], exp=partner)
    swap_last.start()
    out_ref[core] = jnp.where(core == 0, final[0], final[1]).astype(BF16)

    for drain in drains:
        drain()

    def pairs_sent(o, carry):
        pair_copy(o).wait_send()
        return carry

    lax.fori_loop(0, n, pairs_sent, 0)

    def sums_sent(j, carry):
        sum_copy(lax.rem(chip + j, n)).wait_send()
        return carry

    lax.fori_loop(1, n, sums_sent, 0)
    swap.wait_send()
    swap_last.wait_send()
    spot = out_ref.at[1 - core]
    remote(spot, spot, few_send.at[5], few_recv.at[5], exp=partner).wait_recv()


def body(
    queries,
    key_rows,
    value_rows,
    decay_rate,
    residual,
    out_proj,
    routes,
    gate_shares,
    gate_proj,
    up_proj,
    down_proj,
):
    n = lax.axis_size("ctx")
    holders = lax.axis_size("exp")
    count, wide = queries.shape
    heads = decay_rate.shape[0]
    width = wide // heads
    own_rows, slice_width = residual.shape
    part_width = slice_width // 2
    capacity = 2 * own_rows * routes.shape[1] // n
    slots = holders * capacity
    units = gate_proj.shape[1]
    vmem, dma = pltpu.VMEM, pltpu.SemaphoreType.DMA
    on_chip = pl.BlockSpec(memory_space=pltpu.VMEM)
    anywhere = pl.BlockSpec(memory_space=pl.ANY)
    half = n // 2
    ring4, ring3, each = dma((2, half, 4)), dma((2, half, 3)), dma((n,))
    out = pl.pallas_call(
        functools.partial(layer_kernel, n),
        out_shape=jax.ShapeDtypeStruct((2, own_rows, LANES), BF16),
        in_specs=[on_chip] * 3
        + [pl.BlockSpec(memory_space=pltpu.SMEM)]
        + [on_chip] * 4
        + [anywhere] * 3,
        out_specs=on_chip,
        scratch_shapes=[
            vmem((n, 2 * heads, width // 2, width), BF16),
            vmem((n, 4, count // 4, wide), BF16),
            vmem((n, part_width, count), BF16),
            vmem((n, part_width, count), F32),
            vmem((n, part_width, count), BF16),
            vmem((n, part_width, count), BF16),
            vmem((n, part_width, count), BF16),
            vmem((2 * own_rows, slice_width), BF16),
            vmem((2,) + routes.shape[::-1], jnp.int32),
            vmem((2,) + routes.shape[::-1], jnp.int32),
            vmem((LANES, count), BF16),
            vmem((n, 2, capacity, LANES), BF16),
            vmem((n, 2, capacity, LANES), BF16),
            vmem((n, 2, 3, part_width // 3, slots), BF16),
            vmem((n, 4, units // 4, slots), BF16),
            vmem((slice_width, slots), F32),
            vmem((part_width, slots), BF16),
            vmem((part_width, slots), BF16),
            vmem((LANES, slots), BF16),
            vmem((n, 2, capacity, LANES), BF16),
            vmem((n, 2, capacity, LANES), BF16),
            vmem((own_rows, LANES), BF16),
            vmem(gate_proj.shape[1:], BF16),
            vmem(up_proj.shape[1:], BF16),
            vmem(down_proj.shape[1:], BF16),
            vmem((units, slots), F32),
            vmem((units, slots), F32),
            vmem((1, slots), F32),
        ]
        + [ring4] * 4
        + [ring3] * 2
        + [ring4] * 2
        + [ring3] * 2
        + [each] * 8
        + [dma((6,))] * 2
        + [dma((3,))],
        compiler_params=pltpu.CompilerParams(
            collective_id=0, has_side_effects=True, vmem_limit_bytes=56 * 2**20
        ),
        name="layer",
    )(
        queries,
        key_rows,
        value_rows,
        decay_rate,
        residual,
        out_proj.T,
        routes.T,
        gate_shares.T,
        gate_proj,
        up_proj,
        down_proj,
    )
    return jnp.concatenate([out[0, :, :part_width], out[1, :, :part_width]], axis=1)


def solution(mesh):
    in_specs = (
        P("ctx", "exp"),
        P("ctx", "exp"),
        P("ctx", "exp"),
        P("exp"),
        P("exp", "ctx"),
        P("exp", "ctx"),
        P("exp", None),
        P("exp", None),
        P("exp", "ctx", None),
        P("exp", "ctx", None),
        P("exp", "ctx", None),
    )
    out_specs = P("exp", "ctx")
    return jax.shard_map(body, mesh=mesh, in_specs=in_specs, out_specs=out_specs, check_vma=False)
```

```python
import functools
import jax
import jax.numpy as jnp
from jax import lax
from jax.experimental import pallas as pl
from jax.experimental.pallas import tpu as pltpu
from jax.sharding import PartitionSpec as P

MESH = pl.DeviceIdType.MESH
F32 = jnp.float32
BF16 = jnp.bfloat16
BEST = lax.Precision.HIGHEST
LANES = 128


def dot_nt(a, b):
    return lax.dot_general(a, b, (((1,), (1,)), ((), ())), preferred_element_type=F32)


def dot_nn(a, b):
    return jnp.dot(a, b, preferred_element_type=F32)


def unit(rows, cols):
    down = lax.broadcasted_iota(jnp.int32, (rows, cols), 0)
    along = lax.broadcasted_iota(jnp.int32, (rows, cols), 1)
    return (down == along).astype(F32).astype(BF16)


def layer_kernel(
    n,
    q_ref,
    k_ref,
    v_ref,
    rate_ref,
    res_ref,
    proj_ref,
    routes_ref,
    shares_ref,
    gate_hbm,
    up_hbm,
    down_hbm,
    out_ref,
    states,
    attns,
    give,
    mine,
    got,
    passed,
    land,
    res_both,
    routes_both,
    shares_both,
    turned_stream,
    leaving,
    arrived,
    tokens,
    hidden,
    product,
    earlier,
    streams,
    turned_out,
    back,
    home,
    last,
    w_gate,
    w_up,
    w_down,
    gate_sum,
    up_sum,
    square,
    s_send,
    s_recv,
    a_send,
    a_recv,
    t_send,
    t_recv,
    h_send,
    h_recv,
    x_send,
    x_recv,
    pair_send,
    pair_recv,
    sum_send,
    sum_recv,
    go_send,
    go_recv,
    back_send,
    back_recv,
    few_send,
    few_recv,
    w_sem,
):
    me = lax.axis_index("ctx")
    col = lax.axis_index("exp")
    chip = col // 2
    core = lax.rem(col, 2)
    partner = col + 1 - 2 * core
    half = n // 2

    def along(way, steps):
        return lax.rem(me + steps, n) if way == 0 else lax.rem(me - steps + n, n)

    count, wide = q_ref.shape
    heads = rate_ref.shape[0]
    width = wide // heads
    own_rows, slice_width = res_ref.shape
    part_width = slice_width // 2
    slots = hidden.shape[-1]
    capacity = leaving.shape[2]
    lanes_out = n * capacity

    def remote(src, dst, send_sem, recv_sem, **where):
        return pltpu.make_async_remote_copy(
            src_ref=src,
            dst_ref=dst,
            send_sem=send_sem,
            recv_sem=recv_sem,
            device_id=where,
            device_id_type=MESH,
        )

    weights = [
        pltpu.make_async_copy(src.at[0], dst, w_sem.at[i])
        for i, (src, dst) in enumerate(((gate_hbm, w_gate), (up_hbm, w_up), (down_hbm, w_down)))
    ]
    for copy in weights:
        copy.start()

    barrier = pltpu.get_barrier_semaphore()
    for steps in (1, 2):
        for way in range(2):
            peer = along(way, steps)
            pl.semaphore_signal(barrier, inc=1, device_id={"ctx": peer}, device_id_type=MESH)

    holders = 2 * n

    def greet(j, carry):
        peer = lax.rem(col + j, holders)
        pl.semaphore_signal(barrier, inc=1, device_id={"exp": peer}, device_id_type=MESH)
        return carry

    lax.fori_loop(1, holders, greet, 0)

    down_iota = lax.broadcasted_iota(jnp.int32, (count, width), 0).astype(F32)
    right_iota = lax.broadcasted_iota(jnp.int32, (count, width), 1).astype(F32)
    head_at = [slice(h * width, (h + 1) * width) for h in range(heads)]
    for h in range(heads):
        faded = k_ref[:, head_at[h]].astype(F32) * jnp.exp(-rate_ref[h] * (count - down_iota))
        local = jnp.dot(
            faded.T, v_ref[:, head_at[h]].astype(F32), precision=BEST, preferred_element_type=F32
        ).astype(BF16)
        states[me, 2 * h] = local[: width // 2]
        states[me, 2 * h + 1] = local[width // 2 :]
    res_both[pl.ds(pl.multiple_of(core * own_rows, own_rows), own_rows), :] = res_ref[...]
    routes_both[core] = routes_ref[...]
    shares_both[core] = shares_ref[...]
    pl.semaphore_wait(barrier, holders + 3)

    rows_mine = res_both.at[pl.ds(pl.multiple_of(core * own_rows, own_rows), own_rows), :]
    rows_other = res_both.at[pl.ds(pl.multiple_of((1 - core) * own_rows, own_rows), own_rows), :]
    early = [
        (remote(res_ref, rows_mine, few_send.at[0], few_recv.at[0], exp=partner), rows_other),
        (
            remote(routes_ref, routes_both.at[core], few_send.at[1], few_recv.at[1], exp=partner),
            routes_both.at[1 - core],
        ),
        (
            remote(shares_ref, shares_both.at[core], few_send.at[2], few_recv.at[2], exp=partner),
            shares_both.at[1 - core],
        ),
    ]

    def origin_of(way, step):
        return along(1 - way, step)

    def ring(place, chunks, send, recv, work, forward=None, skip=False):
        def hop(way, step, stride, chunk):
            spot = place(origin_of(way, step - stride), chunk)
            sems = (send.at[way, step - 1, chunk], recv.at[way, step - 1, chunk])
            return remote(spot, spot, *sems, ctx=along(way, stride))

        def landed(way, step, chunk):
            spot = place(origin_of(way, step), chunk)
            sems = (send.at[way, step - 1, chunk], recv.at[way, step - 1, chunk])
            return remote(spot, spot, *sems, ctx=along(way, 1))

        every = [(chunk, way) for chunk in range(chunks) for way in range(2)]
        last_hop = [(chunk, way) for chunk, way in every if (chunk < chunks // 2) == (way == 0)]

        def turn(step, even, arriving, far, close):
            for chunk, way in every:
                if (chunk, way) in arriving:
                    landed(way, step, chunk).wait_recv()
                if skip and even and (chunk, way) in far:
                    hop(way, step + 2, 2, chunk).start()
                if (not skip or even) and (chunk, way) in close:
                    hop(way, step + 1, 1, chunk).start()
                if forward is not None and (chunk, way) in arriving:
                    forward(way, step, chunk).start()

        def both(step):
            return [origin_of(0, step), origin_of(1, step)]

        turn(0, True, [], every, every)
        work(0, [me])
        turn(1, False, every, every, every)
        work(1, both(1))

        def middle(i, carry):
            turn(2 * i, True, every, every, every)
            work(2 * i, both(2 * i))
            turn(2 * i + 1, False, every, every, every)
            work(2 * i + 1, both(2 * i + 1))
            return carry

        lax.fori_loop(1, half // 2 - 1, middle, 0)
        turn(half - 2, True, every, last_hop, every)
        work(half - 2, both(half - 2))
        turn(half - 1, False, every, [], last_hop)
        work(half - 1, both(half - 1))
        turn(half, True, last_hop, [], [])
        work(half, [origin_of(0, half)])

        def drain():
            def sent(step, carry):
                for chunk, way in every:
                    landed(way, step, chunk).wait_send()
                return carry

            lax.fori_loop(1, half, sent, 0)
            for chunk, way in last_hop:
                landed(way, half, chunk).wait_send()

        return drain

    lags = down_iota - right_iota
    inner = []

    def inside(step, origins):
        if isinstance(step, int) and step == 0:
            for copy, _ in early:
                copy.start()
            for h in range(heads):
                scores = dot_nt(q_ref[:, head_at[h]], k_ref[:, head_at[h]])
                keep = jnp.where(lags >= 0, jnp.exp(-rate_ref[h] * jnp.maximum(lags, 0.0)), 0.0)
                inner.append(dot_nn((scores * keep).astype(BF16), v_ref[:, head_at[h]]))
            earlier[...] = jnp.zeros_like(earlier)
            return
        for j in origins:
            between = me - 1 - j
            span = jnp.full((1, width), jnp.maximum(between, 0)).astype(F32)
            for h in range(heads):
                fade = jnp.where(between >= 0, jnp.exp(-rate_ref[h] * count * span), 0.0)
                state = states[j, pl.ds(2 * h, 2)].reshape(width, width)
                earlier[h] += fade * state.astype(F32)

    drains = [
        ring(lambda o, c: states.at[o, c], states.shape[1], s_send, s_recv, inside, skip=True)
    ]
    for h in range(heads):
        high = earlier[h].astype(BF16)
        low = (earlier[h] - high.astype(F32)).astype(BF16)
        query = q_ref[:, head_at[h]]
        across = dot_nn(query, high) + dot_nn(query, low)
        mixed = inner[h] + across * jnp.exp(-rate_ref[h] * down_iota)
        scale = lax.rsqrt(jnp.mean(mixed * mixed, axis=-1, keepdims=True) + 1e-06)
        attn = (mixed * scale).astype(BF16)
        piece = count // attns.shape[1]
        for c in range(attns.shape[1]):
            attns[me, c, :, head_at[h]] = attn[c * piece : (c + 1) * piece]

    def pair_copy(o):
        return remote(give.at[o], got.at[o], pair_send.at[o], pair_recv.at[o], exp=partner)

    def sum_copy(o):
        sems = (sum_send.at[o], sum_recv.at[chip])
        return remote(passed.at[o], land.at[chip], *sems, exp=2 * o + core)

    def split(value):
        low, high = value[:part_width], value[part_width:]
        return jnp.where(core == 0, low, high), jnp.where(core == 0, high, low)

    def project(o):
        block = attns[o].reshape(count, wide)
        kept, given = split(dot_nt(proj_ref[...], block))
        mine[o] = kept
        give[o] = given.astype(BF16)
        pair_copy(o).start()

    def hand_on(o):
        pair_copy(o).wait_recv()
        total = (mine[o] + got[o].astype(F32)).astype(BF16)

        @pl.when(o == chip)
        def _():
            land[o] = total

        @pl.when(o != chip)
        def _():
            passed[o] = total
            sum_copy(o).start()

    def out_step(step, origins):
        for o in origins:
            project(o)
        if isinstance(step, int) and step == 1:
            hand_on(me)
        elif not (isinstance(step, int) and step == 0):
            hand_on(origin_of(0, step - 1))
            hand_on(origin_of(1, step - 1))
        if isinstance(step, int) and step == half:
            hand_on(origin_of(0, half))

    drains.append(
        ring(lambda o, c: attns.at[o, c], attns.shape[1], a_send, a_recv, out_step, skip=True)
    )

    for copy, spot in early:
        copy.wait_send()
    for i, (copy, spot) in enumerate(early):
        remote(spot, spot, few_send.at[i], few_recv.at[i], exp=partner).wait_recv()

    lane = lax.broadcasted_iota(jnp.int32, (own_rows, lanes_out), 1)
    expert_of, slot_of = (lane // capacity).astype(F32), lax.rem(lane, capacity).astype(F32)
    upright = unit(own_rows, own_rows)
    before = (
        lax.broadcasted_iota(jnp.int32, (own_rows, own_rows), 0)
        > lax.broadcasted_iota(jnp.int32, (own_rows, own_rows), 1)
    ).astype(F32)
    flip = unit(lanes_out, lanes_out)
    pickers, combiners = [], []
    for b in range(2):
        chosen = dot_nt(upright, routes_both[b].astype(F32).astype(BF16))
        first = (chosen[:, 0:1] == expert_of).astype(F32)
        second = (chosen[:, 1:2] == expert_of).astype(F32)
        named = first + second
        rank = dot_nn(before.astype(BF16), named.astype(BF16))
        placed = jnp.where(rank == slot_of, named, 0.0)
        part = dot_nt(upright, shares_both[b].astype(F32).astype(BF16))
        whole = part[:, 0:1] + part[:, 1:2]
        combiners.append(placed * (first * (part[:, 0:1] / whole) + second * (part[:, 1:2] / whole)))
        pickers.append(dot_nt(flip, placed.astype(BF16)).astype(BF16))

    choose = (
        lax.broadcasted_iota(jnp.int32, (part_width, slice_width), 0) + core * part_width
        == lax.broadcasted_iota(jnp.int32, (part_width, slice_width), 1)
    ).astype(F32)
    start = dot_nt(choose.astype(BF16), res_both[...])

    def sum_landed(p):
        sems = (sum_send.at[p], sum_recv.at[p])
        return remote(land.at[p], land.at[p], *sems, exp=2 * p + core)

    def add_part(j, total):
        p = lax.rem(chip + j, n)

        @pl.when(j > 0)
        def _():
            sum_landed(p).wait_recv()

        return total + land[p].astype(F32)

    stream = lax.fori_loop(0, n, add_part, jnp.zeros((part_width, count), F32))
    stream = (stream + start).astype(BF16)
    turned_stream[pl.ds(part_width, LANES - part_width), :] = jnp.zeros(
        (LANES - part_width, count), BF16
    )
    turned_stream[pl.ds(0, part_width), :] = stream
    by_token = dot_nt(unit(count, count), turned_stream[...]).astype(BF16)
    by_block = [by_token[:own_rows], by_token[own_rows:]]
    last[...] = jnp.where(core == 0, by_block[1].astype(F32), by_block[0].astype(F32)).astype(BF16)
    streams[core] = jnp.where(
        core == 0, by_block[0].astype(F32), by_block[1].astype(F32)
    ).astype(BF16)
    swap = remote(last, streams.at[core], few_send.at[4], few_recv.at[4], exp=partner)

    def exchange(src, dst, send, recv):
        def outward(j):
            p = lax.rem(chip + j, n)
            return remote(src.at[p], dst.at[chip], send.at[p], recv.at[chip], exp=2 * p + core)

        def inward(j):
            p = lax.rem(chip + j, n)
            return remote(dst.at[p], dst.at[p], send.at[p], recv.at[p], exp=2 * p + core)

        def launch(j, carry):
            outward(j).start()
            return carry

        def finish(j, carry):
            inward(j).wait_recv()
            return carry

        def sent(j, carry):
            outward(j).wait_send()
            return carry

        lax.fori_loop(1, n, launch, 0)
        dst[chip] = src[chip]
        lax.fori_loop(1, n, finish, 0)
        drains.append(lambda: lax.fori_loop(1, n, sent, 0))

    for b in range(2):
        picked = dot_nn(pickers[b], by_block[b]).astype(BF16)
        leaving[:, b] = picked.reshape(n, capacity, LANES)
    exchange(leaving, arrived, go_send, go_recv)
    swap.start()

    turned = dot_nt(unit(part_width, LANES), arrived[...].reshape(slots, LANES)).astype(BF16)
    chunks = tokens.shape[2]
    piece = part_width // chunks
    for c in range(chunks):
        tokens[me, core, c] = turned[c * piece : (c + 1) * piece]

    def hand_across(way, step, chunk):
        spot = tokens.at[origin_of(way, step), core, chunk]
        sems = (x_send.at[way, step - 1, chunk], x_recv.at[way, step - 1, chunk])
        return remote(spot, spot, *sems, exp=partner)

    def handed(way, step, chunk):
        spot = tokens.at[origin_of(way, step), 1 - core, chunk]
        sems = (x_send.at[way, step - 1, chunk], x_recv.at[way, step - 1, chunk])
        return remote(spot, spot, *sems, exp=partner)

    def own_across(side):
        spot = tokens.at[me, side]
        return remote(spot, spot, few_send.at[3], few_recv.at[3], exp=partner)

    ways = [(chunk, way) for chunk in range(chunks) for way in range(2)]
    ending = [(chunk, way) for chunk, way in ways if (chunk < chunks // 2) == (way == 0)]

    def multiply(step, arrivals):
        for chunk, way in arrivals:
            handed(way, step, chunk).wait_recv()
        odd = lax.rem(me + step, 2) == 1
        base = lax.rem(jnp.where(odd, me + step - 1, me - step + n), n)
        block = tokens[pl.ds(base, 2)].reshape(2 * slice_width, slots)
        span = pl.ds(pl.multiple_of(base * slice_width, 2 * slice_width), 2 * slice_width)
        gate_sum[...] += dot_nn(w_gate[:, span], block)
        up_sum[...] += dot_nn(w_up[:, span], block)
        wide_block = block.astype(F32)
        square[...] += jnp.sum(wide_block * wide_block, axis=0, keepdims=True)

    def token_step(step, origins):
        if isinstance(step, int) and step == 0:
            own_across(core).start()
            gate_sum[...] = jnp.zeros_like(gate_sum)
            up_sum[...] = jnp.zeros_like(up_sum)
            square[...] = jnp.zeros_like(square)
        elif isinstance(step, int) and step == 1:
            for copy in weights:
                copy.wait()
            own_across(1 - core).wait_recv()
        else:
            multiply(step - 1, ways)

    drains.append(
        ring(lambda o, c: tokens.at[o, core, c], chunks, t_send, t_recv, token_step, hand_across)
    )
    multiply(half, ending)

    def across_sent():
        def sent(step, carry):
            for chunk, way in ways:
                hand_across(way, step, chunk).wait_send()
            return carry

        lax.fori_loop(1, half, sent, 0)
        for chunk, way in ending:
            hand_across(way, half, chunk).wait_send()
        own_across(core).wait_send()

    drains.append(across_sent)

    scale = lax.rsqrt(square[...] / (n * slice_width) + 1e-06)
    gate = gate_sum[...] * scale
    upper = up_sum[...] * scale
    unit_rows = (gate / (1.0 + jnp.exp(-gate)) * upper).astype(BF16)
    units = unit_rows.shape[0]
    piece = units // hidden.shape[1]
    for c in range(hidden.shape[1]):
        hidden[me, c] = unit_rows[c * piece : (c + 1) * piece]

    def down_step(step, origins):
        for o in origins:
            at = pl.ds(pl.multiple_of(o * units, units), units)
            term = dot_nn(w_down[:, at], hidden[o].reshape(units, slots))
            if isinstance(step, int) and step == 0:
                product[...] = term
            else:
                product[...] += term

    drains.append(ring(lambda o, c: hidden.at[o, c], hidden.shape[1], h_send, h_recv, down_step))

    for f in range(2):
        turned_out[f, pl.ds(part_width, LANES - part_width), :] = jnp.zeros(
            (LANES - part_width, slots), BF16
        )
        turned_out[f, pl.ds(0, part_width), :] = product[
            pl.ds(f * part_width, part_width), :
        ].astype(BF16)
    owners = LANES // capacity
    for j in range(slots // LANES):
        for f in range(2):
            rows = dot_nt(unit(LANES, LANES), turned_out[f, :, j * LANES : (j + 1) * LANES])
            back[pl.ds(j * owners, owners), f] = rows.astype(BF16).reshape(owners, capacity, LANES)

    def homeward(j):
        peer = lax.rem(col + j, holders)
        sems = (back_send.at[peer], back_recv.at[col])
        return remote(back.at[peer], home.at[col], *sems, exp=peer)

    def come_home(j):
        peer = lax.rem(col + j, holders)
        sems = (back_send.at[peer], back_recv.at[peer])
        return remote(home.at[peer], home.at[peer], *sems, exp=peer)

    def launch_home(j, carry):
        homeward(j).start()
        return carry

    def finish_home(j, carry):
        come_home(j).wait_recv()
        return carry

    def home_sent(j, carry):
        homeward(j).wait_send()
        return carry

    lax.fori_loop(1, holders, launch_home, 0)
    home[col] = back[col]
    spot = streams.at[1 - core]
    remote(spot, spot, few_send.at[4], few_recv.at[4], exp=partner).wait_recv()
    combiner = jnp.where(core == 0, combiners[0], combiners[1])
    lax.fori_loop(1, holders, finish_home, 0)
    for f in range(2):
        outs = home[:, f].reshape(n, 2, capacity, LANES).astype(F32)
        outs = (outs[:, 0] + outs[:, 1]).astype(BF16).astype(F32).reshape(lanes_out, LANES)
        mixed = jnp.dot(combiner, outs, precision=BEST, preferred_element_type=F32)
        out_ref[f] = (streams[f].astype(F32) + mixed).astype(BF16)

    lax.fori_loop(1, holders, home_sent, 0)
    for drain in drains:
        drain()

    def pairs_sent(o, carry):
        pair_copy(o).wait_send()
        return carry

    lax.fori_loop(0, n, pairs_sent, 0)

    def sums_sent(j, carry):
        sum_copy(lax.rem(chip + j, n)).wait_send()
        return carry

    lax.fori_loop(1, n, sums_sent, 0)
    swap.wait_send()


def body(
    queries,
    key_rows,
    value_rows,
    decay_rate,
    residual,
    out_proj,
    routes,
    gate_shares,
    gate_proj,
    up_proj,
    down_proj,
):
    n = lax.axis_size("ctx")
    holders = lax.axis_size("exp")
    count, wide = queries.shape
    heads = decay_rate.shape[0]
    width = wide // heads
    own_rows, slice_width = residual.shape
    part_width = slice_width // 2
    capacity = 2 * own_rows * routes.shape[1] // n
    slots = holders * capacity
    units = gate_proj.shape[1]
    vmem, dma = pltpu.VMEM, pltpu.SemaphoreType.DMA
    on_chip = pl.BlockSpec(memory_space=pltpu.VMEM)
    anywhere = pl.BlockSpec(memory_space=pl.ANY)
    half = n // 2
    ring4, ring3, each = dma((2, half, 4)), dma((2, half, 3)), dma((n,))
    out = pl.pallas_call(
        functools.partial(layer_kernel, n),
        out_shape=jax.ShapeDtypeStruct((2, own_rows, LANES), BF16),
        in_specs=[on_chip] * 3
        + [pl.BlockSpec(memory_space=pltpu.SMEM)]
        + [on_chip] * 4
        + [anywhere] * 3,
        out_specs=on_chip,
        scratch_shapes=[
            vmem((n, 2 * heads, width // 2, width), BF16),
            vmem((n, 4, count // 4, wide), BF16),
            vmem((n, part_width, count), BF16),
            vmem((n, part_width, count), F32),
            vmem((n, part_width, count), BF16),
            vmem((n, part_width, count), BF16),
            vmem((n, part_width, count), BF16),
            vmem((2 * own_rows, slice_width), BF16),
            vmem((2,) + routes.shape[::-1], jnp.int32),
            vmem((2,) + routes.shape[::-1], jnp.int32),
            vmem((LANES, count), BF16),
            vmem((n, 2, capacity, LANES), BF16),
            vmem((n, 2, capacity, LANES), BF16),
            vmem((n, 2, 3, part_width // 3, slots), BF16),
            vmem((n, 4, units // 4, slots), BF16),
            vmem((slice_width, slots), F32),
            vmem((heads, width, width), F32),
            vmem((2, own_rows, LANES), BF16),
            vmem((2, LANES, slots), BF16),
            vmem((holders, 2, capacity, LANES), BF16),
            vmem((holders, 2, capacity, LANES), BF16),
            vmem((own_rows, LANES), BF16),
            vmem(gate_proj.shape[1:], BF16),
            vmem(up_proj.shape[1:], BF16),
            vmem(down_proj.shape[1:], BF16),
            vmem((units, slots), F32),
            vmem((units, slots), F32),
            vmem((1, slots), F32),
        ]
        + [ring4] * 4
        + [ring3] * 2
        + [ring4] * 2
        + [ring3] * 2
        + [each] * 6
        + [dma((holders,))] * 2
        + [dma((5,))] * 2
        + [dma((3,))],
        compiler_params=pltpu.CompilerParams(
            collective_id=0, has_side_effects=True, vmem_limit_bytes=56 * 2**20
        ),
        name="layer",
    )(
        queries,
        key_rows,
        value_rows,
        decay_rate,
        residual,
        out_proj.T,
        routes.T,
        gate_shares.T,
        gate_proj,
        up_proj,
        down_proj,
    )
    return jnp.concatenate([out[0, :, :part_width], out[1, :, :part_width]], axis=1)


def solution(mesh):
    in_specs = (
        P("ctx", "exp"),
        P("ctx", "exp"),
        P("ctx", "exp"),
        P("exp"),
        P("exp", "ctx"),
        P("exp", "ctx"),
        P("exp", None),
        P("exp", None),
        P("exp", "ctx", None),
        P("exp", "ctx", None),
        P("exp", "ctx", None),
    )
    out_specs = P("exp", "ctx")
    return jax.shard_map(body, mesh=mesh, in_specs=in_specs, out_specs=out_specs, check_vma=False)
```

```python
import functools
import jax
import jax.numpy as jnp
from jax import lax
from jax.experimental import pallas as pl
from jax.experimental.pallas import tpu as pltpu
from jax.sharding import PartitionSpec as P

MESH = pl.DeviceIdType.MESH
F32 = jnp.float32
BF16 = jnp.bfloat16
BEST = lax.Precision.HIGHEST
LANES = 128


def dot_nt(a, b):
    return lax.dot_general(a, b, (((1,), (1,)), ((), ())), preferred_element_type=F32)


def dot_nn(a, b):
    return jnp.dot(a, b, preferred_element_type=F32)


def unit(rows, cols):
    down = lax.broadcasted_iota(jnp.int32, (rows, cols), 0)
    along = lax.broadcasted_iota(jnp.int32, (rows, cols), 1)
    return (down == along).astype(F32).astype(BF16)


def layer_kernel(
    n,
    q_ref,
    k_ref,
    v_ref,
    rate_ref,
    res_ref,
    proj_ref,
    routes_ref,
    shares_ref,
    gate_hbm,
    up_hbm,
    down_hbm,
    out_ref,
    states,
    attns,
    give,
    mine,
    got,
    passed,
    land,
    res_both,
    routes_both,
    shares_both,
    turned_stream,
    leaving,
    arrived,
    tokens,
    hidden,
    product,
    earlier,
    streams,
    turned_out,
    terms,
    other_terms,
    back,
    home,
    last,
    w_gate,
    w_up,
    w_down,
    gate_sum,
    up_sum,
    square,
    s_send,
    s_recv,
    a_send,
    a_recv,
    t_send,
    t_recv,
    h_send,
    h_recv,
    x_send,
    x_recv,
    pair_send,
    pair_recv,
    sum_send,
    sum_recv,
    go_send,
    go_recv,
    back_send,
    back_recv,
    few_send,
    few_recv,
    w_sem,
):
    me = lax.axis_index("ctx")
    col = lax.axis_index("exp")
    chip = col // 2
    core = lax.rem(col, 2)
    partner = col + 1 - 2 * core
    half = n // 2

    def along(way, steps):
        return lax.rem(me + steps, n) if way == 0 else lax.rem(me - steps + n, n)

    count, wide = q_ref.shape
    heads = rate_ref.shape[0]
    width = wide // heads
    own_rows, slice_width = res_ref.shape
    part_width = slice_width // 2
    slots = hidden.shape[-1]
    capacity = leaving.shape[2]
    lanes_out = n * capacity

    def remote(src, dst, send_sem, recv_sem, **where):
        return pltpu.make_async_remote_copy(
            src_ref=src,
            dst_ref=dst,
            send_sem=send_sem,
            recv_sem=recv_sem,
            device_id=where,
            device_id_type=MESH,
        )

    weights = [
        pltpu.make_async_copy(src.at[0], dst, w_sem.at[i])
        for i, (src, dst) in enumerate(((gate_hbm, w_gate), (up_hbm, w_up), (down_hbm, w_down)))
    ]
    for copy in weights:
        copy.start()

    barrier = pltpu.get_barrier_semaphore()
    for steps in (1, 2):
        for way in range(2):
            peer = along(way, steps)
            pl.semaphore_signal(barrier, inc=1, device_id={"ctx": peer}, device_id_type=MESH)

    pl.semaphore_signal(barrier, inc=1, device_id={"exp": partner}, device_id_type=MESH)

    def greet(j, carry):
        peer = 2 * lax.rem(chip + j, n) + core
        pl.semaphore_signal(barrier, inc=1, device_id={"exp": peer}, device_id_type=MESH)
        return carry

    lax.fori_loop(1, n, greet, 0)

    down_iota = lax.broadcasted_iota(jnp.int32, (count, width), 0).astype(F32)
    right_iota = lax.broadcasted_iota(jnp.int32, (count, width), 1).astype(F32)
    head_at = [slice(h * width, (h + 1) * width) for h in range(heads)]
    for h in range(heads):
        faded = k_ref[:, head_at[h]].astype(F32) * jnp.exp(-rate_ref[h] * (count - down_iota))
        local = jnp.dot(
            faded.T, v_ref[:, head_at[h]].astype(F32), precision=BEST, preferred_element_type=F32
        ).astype(BF16)
        states[me, 2 * h] = local[: width // 2]
        states[me, 2 * h + 1] = local[width // 2 :]
    res_both[pl.ds(pl.multiple_of(core * own_rows, own_rows), own_rows), :] = res_ref[...]
    routes_both[core] = routes_ref[...]
    shares_both[core] = shares_ref[...]
    pl.semaphore_wait(barrier, n + 4)

    rows_mine = res_both.at[pl.ds(pl.multiple_of(core * own_rows, own_rows), own_rows), :]
    rows_other = res_both.at[pl.ds(pl.multiple_of((1 - core) * own_rows, own_rows), own_rows), :]
    early = [
        (remote(res_ref, rows_mine, few_send.at[0], few_recv.at[0], exp=partner), rows_other),
        (
            remote(routes_ref, routes_both.at[core], few_send.at[1], few_recv.at[1], exp=partner),
            routes_both.at[1 - core],
        ),
        (
            remote(shares_ref, shares_both.at[core], few_send.at[2], few_recv.at[2], exp=partner),
            shares_both.at[1 - core],
        ),
    ]

    def origin_of(way, step):
        return along(1 - way, step)

    def ring(place, chunks, send, recv, work, forward=None, skip=False):
        def hop(way, step, stride, chunk):
            spot = place(origin_of(way, step - stride), chunk)
            sems = (send.at[way, step - 1, chunk], recv.at[way, step - 1, chunk])
            return remote(spot, spot, *sems, ctx=along(way, stride))

        def landed(way, step, chunk):
            spot = place(origin_of(way, step), chunk)
            sems = (send.at[way, step - 1, chunk], recv.at[way, step - 1, chunk])
            return remote(spot, spot, *sems, ctx=along(way, 1))

        every = [(chunk, way) for chunk in range(chunks) for way in range(2)]
        last_hop = [(chunk, way) for chunk, way in every if (chunk < chunks // 2) == (way == 0)]

        def turn(step, even, arriving, far, close):
            for chunk, way in every:
                if (chunk, way) in arriving:
                    landed(way, step, chunk).wait_recv()
                if skip and even and (chunk, way) in far:
                    hop(way, step + 2, 2, chunk).start()
                if (not skip or even) and (chunk, way) in close:
                    hop(way, step + 1, 1, chunk).start()
                if forward is not None and (chunk, way) in arriving:
                    forward(way, step, chunk).start()

        def both(step):
            return [origin_of(0, step), origin_of(1, step)]

        turn(0, True, [], every, every)
        work(0, [me])
        turn(1, False, every, every, every)
        work(1, both(1))

        def middle(i, carry):
            turn(2 * i, True, every, every, every)
            work(2 * i, both(2 * i))
            turn(2 * i + 1, False, every, every, every)
            work(2 * i + 1, both(2 * i + 1))
            return carry

        lax.fori_loop(1, half // 2 - 1, middle, 0)
        turn(half - 2, True, every, last_hop, every)
        work(half - 2, both(half - 2))
        turn(half - 1, False, every, [], last_hop)
        work(half - 1, both(half - 1))
        turn(half, True, last_hop, [], [])
        work(half, [origin_of(0, half)])

        def drain():
            def sent(step, carry):
                for chunk, way in every:
                    landed(way, step, chunk).wait_send()
                return carry

            lax.fori_loop(1, half, sent, 0)
            for chunk, way in last_hop:
                landed(way, half, chunk).wait_send()

        return drain

    lags = down_iota - right_iota
    inner = []

    def inside(step, origins):
        if isinstance(step, int) and step == 0:
            for copy, _ in early:
                copy.start()
            for h in range(heads):
                scores = dot_nt(q_ref[:, head_at[h]], k_ref[:, head_at[h]])
                keep = jnp.where(lags >= 0, jnp.exp(-rate_ref[h] * jnp.maximum(lags, 0.0)), 0.0)
                inner.append(dot_nn((scores * keep).astype(BF16), v_ref[:, head_at[h]]))
            earlier[...] = jnp.zeros_like(earlier)
            return
        for j in origins:
            between = me - 1 - j
            span = jnp.full((1, width), jnp.maximum(between, 0)).astype(F32)
            for h in range(heads):
                fade = jnp.where(between >= 0, jnp.exp(-rate_ref[h] * count * span), 0.0)
                state = states[j, pl.ds(2 * h, 2)].reshape(width, width)
                earlier[h] += fade * state.astype(F32)

    drains = [
        ring(lambda o, c: states.at[o, c], states.shape[1], s_send, s_recv, inside, skip=True)
    ]
    for h in range(heads):
        high = earlier[h].astype(BF16)
        low = (earlier[h] - high.astype(F32)).astype(BF16)
        query = q_ref[:, head_at[h]]
        across = dot_nn(query, high) + dot_nn(query, low)
        mixed = inner[h] + across * jnp.exp(-rate_ref[h] * down_iota)
        scale = lax.rsqrt(jnp.mean(mixed * mixed, axis=-1, keepdims=True) + 1e-06)
        attn = (mixed * scale).astype(BF16)
        piece = count // attns.shape[1]
        for c in range(attns.shape[1]):
            attns[me, c, :, head_at[h]] = attn[c * piece : (c + 1) * piece]

    def pair_copy(o):
        return remote(give.at[o], got.at[o], pair_send.at[o], pair_recv.at[o], exp=partner)

    def sum_copy(o):
        sems = (sum_send.at[o], sum_recv.at[chip])
        return remote(passed.at[o], land.at[chip], *sems, exp=2 * o + core)

    def split(value):
        low, high = value[:part_width], value[part_width:]
        return jnp.where(core == 0, low, high), jnp.where(core == 0, high, low)

    def project(o):
        block = attns[o].reshape(count, wide)
        kept, given = split(dot_nt(proj_ref[...], block))
        mine[o] = kept
        give[o] = given.astype(BF16)
        pair_copy(o).start()

    def hand_on(o):
        pair_copy(o).wait_recv()
        total = (mine[o] + got[o].astype(F32)).astype(BF16)

        @pl.when(o == chip)
        def _():
            land[o] = total

        @pl.when(o != chip)
        def _():
            passed[o] = total
            sum_copy(o).start()

    def out_step(step, origins):
        for o in origins:
            project(o)
        if isinstance(step, int) and step == 1:
            hand_on(me)
        elif not (isinstance(step, int) and step == 0):
            hand_on(origin_of(0, step - 1))
            hand_on(origin_of(1, step - 1))
        if isinstance(step, int) and step == half:
            hand_on(origin_of(0, half))

    drains.append(
        ring(lambda o, c: attns.at[o, c], attns.shape[1], a_send, a_recv, out_step, skip=True)
    )

    for copy, spot in early:
        copy.wait_send()
    for i, (copy, spot) in enumerate(early):
        remote(spot, spot, few_send.at[i], few_recv.at[i], exp=partner).wait_recv()

    lane = lax.broadcasted_iota(jnp.int32, (own_rows, lanes_out), 1)
    expert_of, slot_of = (lane // capacity).astype(F32), lax.rem(lane, capacity).astype(F32)
    upright = unit(own_rows, own_rows)
    before = (
        lax.broadcasted_iota(jnp.int32, (own_rows, own_rows), 0)
        > lax.broadcasted_iota(jnp.int32, (own_rows, own_rows), 1)
    ).astype(F32)
    flip = unit(lanes_out, lanes_out)
    pickers, combiners = [], []
    for b in range(2):
        chosen = dot_nt(upright, routes_both[b].astype(F32).astype(BF16))
        first = (chosen[:, 0:1] == expert_of).astype(F32)
        second = (chosen[:, 1:2] == expert_of).astype(F32)
        named = first + second
        rank = dot_nn(before.astype(BF16), named.astype(BF16))
        placed = jnp.where(rank == slot_of, named, 0.0)
        part = dot_nt(upright, shares_both[b].astype(F32).astype(BF16))
        whole = part[:, 0:1] + part[:, 1:2]
        combiners.append(placed * (first * (part[:, 0:1] / whole) + second * (part[:, 1:2] / whole)))
        pickers.append(dot_nt(flip, placed.astype(BF16)).astype(BF16))

    choose = (
        lax.broadcasted_iota(jnp.int32, (part_width, slice_width), 0) + core * part_width
        == lax.broadcasted_iota(jnp.int32, (part_width, slice_width), 1)
    ).astype(F32)
    start = dot_nt(choose.astype(BF16), res_both[...])

    def sum_landed(p):
        sems = (sum_send.at[p], sum_recv.at[p])
        return remote(land.at[p], land.at[p], *sems, exp=2 * p + core)

    def add_part(j, total):
        p = lax.rem(chip + j, n)

        @pl.when(j > 0)
        def _():
            sum_landed(p).wait_recv()

        return total + land[p].astype(F32)

    stream = lax.fori_loop(0, n, add_part, jnp.zeros((part_width, count), F32))
    stream = (stream + start).astype(BF16)
    turned_stream[pl.ds(part_width, LANES - part_width), :] = jnp.zeros(
        (LANES - part_width, count), BF16
    )
    turned_stream[pl.ds(0, part_width), :] = stream
    by_token = dot_nt(unit(count, count), turned_stream[...]).astype(BF16)
    by_block = [by_token[:own_rows], by_token[own_rows:]]
    last[...] = jnp.where(core == 0, by_block[1].astype(F32), by_block[0].astype(F32)).astype(BF16)
    streams[core] = jnp.where(
        core == 0, by_block[0].astype(F32), by_block[1].astype(F32)
    ).astype(BF16)
    swap = remote(last, streams.at[core], few_send.at[4], few_recv.at[4], exp=partner)

    def exchange(src, dst, send, recv):
        def outward(j):
            p = lax.rem(chip + j, n)
            return remote(src.at[p], dst.at[chip], send.at[p], recv.at[chip], exp=2 * p + core)

        def inward(j):
            p = lax.rem(chip + j, n)
            return remote(dst.at[p], dst.at[p], send.at[p], recv.at[p], exp=2 * p + core)

        def launch(j, carry):
            outward(j).start()
            return carry

        def finish(j, carry):
            inward(j).wait_recv()
            return carry

        def sent(j, carry):
            outward(j).wait_send()
            return carry

        lax.fori_loop(1, n, launch, 0)
        dst[chip] = src[chip]
        lax.fori_loop(1, n, finish, 0)
        drains.append(lambda: lax.fori_loop(1, n, sent, 0))

    for b in range(2):
        picked = dot_nn(pickers[b], by_block[b]).astype(BF16)
        leaving[:, b] = picked.reshape(n, capacity, LANES)
    exchange(leaving, arrived, go_send, go_recv)
    swap.start()

    turned = dot_nt(unit(part_width, LANES), arrived[...].reshape(slots, LANES)).astype(BF16)
    chunks = tokens.shape[2]
    piece = part_width // chunks
    for c in range(chunks):
        tokens[me, core, c] = turned[c * piece : (c + 1) * piece]

    def hand_across(way, step, chunk):
        spot = tokens.at[origin_of(way, step), core, chunk]
        sems = (x_send.at[way, step - 1, chunk], x_recv.at[way, step - 1, chunk])
        return remote(spot, spot, *sems, exp=partner)

    def handed(way, step, chunk):
        spot = tokens.at[origin_of(way, step), 1 - core, chunk]
        sems = (x_send.at[way, step - 1, chunk], x_recv.at[way, step - 1, chunk])
        return remote(spot, spot, *sems, exp=partner)

    def own_across(side):
        spot = tokens.at[me, side]
        return remote(spot, spot, few_send.at[3], few_recv.at[3], exp=partner)

    ways = [(chunk, way) for chunk in range(chunks) for way in range(2)]
    ending = [(chunk, way) for chunk, way in ways if (chunk < chunks // 2) == (way == 0)]

    def multiply(step, arrivals):
        for chunk, way in arrivals:
            handed(way, step, chunk).wait_recv()
        odd = lax.rem(me + step, 2) == 1
        base = lax.rem(jnp.where(odd, me + step - 1, me - step + n), n)
        block = tokens[pl.ds(base, 2)].reshape(2 * slice_width, slots)
        span = pl.ds(pl.multiple_of(base * slice_width, 2 * slice_width), 2 * slice_width)
        gate_sum[...] += dot_nn(w_gate[:, span], block)
        up_sum[...] += dot_nn(w_up[:, span], block)
        wide_block = block.astype(F32)
        square[...] += jnp.sum(wide_block * wide_block, axis=0, keepdims=True)

    def token_step(step, origins):
        if isinstance(step, int) and step == 0:
            own_across(core).start()
            gate_sum[...] = jnp.zeros_like(gate_sum)
            up_sum[...] = jnp.zeros_like(up_sum)
            square[...] = jnp.zeros_like(square)
        elif isinstance(step, int) and step == 1:
            for copy in weights:
                copy.wait()
            own_across(1 - core).wait_recv()
        else:
            multiply(step - 1, ways)

    drains.append(
        ring(lambda o, c: tokens.at[o, core, c], chunks, t_send, t_recv, token_step, hand_across)
    )
    multiply(half, ending)

    def across_sent():
        def sent(step, carry):
            for chunk, way in ways:
                hand_across(way, step, chunk).wait_send()
            return carry

        lax.fori_loop(1, half, sent, 0)
        for chunk, way in ending:
            hand_across(way, half, chunk).wait_send()
        own_across(core).wait_send()

    drains.append(across_sent)

    scale = lax.rsqrt(square[...] / (n * slice_width) + 1e-06)
    gate = gate_sum[...] * scale
    upper = up_sum[...] * scale
    unit_rows = (gate / (1.0 + jnp.exp(-gate)) * upper).astype(BF16)
    units = unit_rows.shape[0]
    piece = units // hidden.shape[1]
    for c in range(hidden.shape[1]):
        hidden[me, c] = unit_rows[c * piece : (c + 1) * piece]

    def down_step(step, origins):
        for o in origins:
            at = pl.ds(pl.multiple_of(o * units, units), units)
            term = dot_nn(w_down[:, at], hidden[o].reshape(units, slots))
            if isinstance(step, int) and step == 0:
                product[...] = term
            else:
                product[...] += term

    drains.append(ring(lambda o, c: hidden.at[o, c], hidden.shape[1], h_send, h_recv, down_step))

    for f in range(2):
        turned_out[f, pl.ds(part_width, LANES - part_width), :] = jnp.zeros(
            (LANES - part_width, slots), BF16
        )
        turned_out[f, pl.ds(0, part_width), :] = product[
            pl.ds(f * part_width, part_width), :
        ].astype(BF16)
    owners = LANES // (2 * capacity)
    for j in range(slots // LANES):
        for f in range(2):
            rows = dot_nt(unit(LANES, LANES), turned_out[f, :, j * LANES : (j + 1) * LANES])
            rows = rows.astype(BF16).reshape(owners, 2, capacity, LANES)
            for b in range(2):
                terms[b, pl.ds(j * owners, owners), f] = rows[:, b]
    swap_terms = remote(
        terms.at[1 - core], other_terms, few_send.at[5], few_recv.at[5], exp=partner
    )
    swap_terms.start()
    spot = streams.at[1 - core]
    remote(spot, spot, few_send.at[4], few_recv.at[4], exp=partner).wait_recv()
    combiner = jnp.where(core == 0, combiners[0], combiners[1])
    swap_terms.wait_recv()
    back[...] = (terms[core].astype(F32) + other_terms[...].astype(F32)).astype(BF16)
    exchange(back, home, back_send, back_recv)

    result = 0.0
    for f in range(2):
        outs = home[:, f].reshape(lanes_out, LANES).astype(F32)
        mixed = jnp.dot(combiner, outs, precision=BEST, preferred_element_type=F32)
        value = (streams[f].astype(F32) + mixed).astype(BF16)
        across = lax.broadcasted_iota(jnp.int32, (LANES, slice_width), 0)
        column = lax.broadcasted_iota(jnp.int32, (LANES, slice_width), 1)
        spread = (across + f * part_width == column) & (across < part_width)
        result += dot_nn(value, spread.astype(F32).astype(BF16))
    out_ref[...] = result.astype(BF16)

    for drain in drains:
        drain()

    def pairs_sent(o, carry):
        pair_copy(o).wait_send()
        return carry

    lax.fori_loop(0, n, pairs_sent, 0)

    def sums_sent(j, carry):
        sum_copy(lax.rem(chip + j, n)).wait_send()
        return carry

    lax.fori_loop(1, n, sums_sent, 0)
    swap.wait_send()
    swap_terms.wait_send()


def body(
    queries,
    key_rows,
    value_rows,
    decay_rate,
    residual,
    out_proj,
    routes,
    gate_shares,
    gate_proj,
    up_proj,
    down_proj,
):
    n = lax.axis_size("ctx")
    holders = lax.axis_size("exp")
    count, wide = queries.shape
    heads = decay_rate.shape[0]
    width = wide // heads
    own_rows, slice_width = residual.shape
    part_width = slice_width // 2
    capacity = 2 * own_rows * routes.shape[1] // n
    slots = holders * capacity
    units = gate_proj.shape[1]
    vmem, dma = pltpu.VMEM, pltpu.SemaphoreType.DMA
    on_chip = pl.BlockSpec(memory_space=pltpu.VMEM)
    anywhere = pl.BlockSpec(memory_space=pl.ANY)
    half = n // 2
    ring4, ring3, each = dma((2, half, 4)), dma((2, half, 3)), dma((n,))
    out = pl.pallas_call(
        functools.partial(layer_kernel, n),
        out_shape=jax.ShapeDtypeStruct((own_rows, slice_width), BF16),
        in_specs=[on_chip] * 3
        + [pl.BlockSpec(memory_space=pltpu.SMEM)]
        + [on_chip] * 4
        + [anywhere] * 3,
        out_specs=on_chip,
        scratch_shapes=[
            vmem((n, 2 * heads, width // 2, width), BF16),
            vmem((n, 4, count // 4, wide), BF16),
            vmem((n, part_width, count), BF16),
            vmem((n, part_width, count), F32),
            vmem((n, part_width, count), BF16),
            vmem((n, part_width, count), BF16),
            vmem((n, part_width, count), BF16),
            vmem((2 * own_rows, slice_width), BF16),
            vmem((2,) + routes.shape[::-1], jnp.int32),
            vmem((2,) + routes.shape[::-1], jnp.int32),
            vmem((LANES, count), BF16),
            vmem((n, 2, capacity, LANES), BF16),
            vmem((n, 2, capacity, LANES), BF16),
            vmem((n, 2, 3, part_width // 3, slots), BF16),
            vmem((n, 4, units // 4, slots), BF16),
            vmem((slice_width, slots), F32),
            vmem((heads, width, width), F32),
            vmem((2, own_rows, LANES), BF16),
            vmem((2, LANES, slots), BF16),
            vmem((2, n, 2, capacity, LANES), BF16),
            vmem((n, 2, capacity, LANES), BF16),
            vmem((n, 2, capacity, LANES), BF16),
            vmem((n, 2, capacity, LANES), BF16),
            vmem((own_rows, LANES), BF16),
            vmem(gate_proj.shape[1:], BF16),
            vmem(up_proj.shape[1:], BF16),
            vmem(down_proj.shape[1:], BF16),
            vmem((units, slots), F32),
            vmem((units, slots), F32),
            vmem((1, slots), F32),
        ]
        + [ring4] * 4
        + [ring3] * 2
        + [ring4] * 2
        + [ring3] * 2
        + [each] * 8
        + [dma((6,))] * 2
        + [dma((3,))],
        compiler_params=pltpu.CompilerParams(
            collective_id=0, has_side_effects=True, vmem_limit_bytes=56 * 2**20
        ),
        name="layer",
    )(
        queries,
        key_rows,
        value_rows,
        decay_rate,
        residual,
        out_proj.T,
        routes.T,
        gate_shares.T,
        gate_proj,
        up_proj,
        down_proj,
    )
    return out


def solution(mesh):
    in_specs = (
        P("ctx", "exp"),
        P("ctx", "exp"),
        P("ctx", "exp"),
        P("exp"),
        P("exp", "ctx"),
        P("exp", "ctx"),
        P("exp", None),
        P("exp", None),
        P("exp", "ctx", None),
        P("exp", "ctx", None),
        P("exp", "ctx", None),
    )
    out_specs = P("exp", "ctx")
    return jax.shard_map(body, mesh=mesh, in_specs=in_specs, out_specs=out_specs, check_vma=False)
```
